768 devices in a mesh: ctx: 24 (over z, core), head: 32 (over x, y).
Axes of the slice: x: 4, y: 8, z: 12, core: 2. Of those that a mesh axis runs over, the one named last changes fastest.
Arguments:
- queries: bfloat16 [12288, 8192], P('ctx', 'head'), may hold values from -24 to 24, as said below
- keys: bfloat16 [12288, 1024], P('ctx'), may hold values from -24 to 24
- values: bfloat16 [12288, 1024], P('ctx'), may hold values from -6 to 6
- out_grad: bfloat16 [12288, 8192], P('ctx', 'head'), may hold values from -6 to 6
- doc_start: int32 [12288], P('ctx'), may hold values from 0 to 12287, as said below
Outputs:
- attn_out: bfloat16 [12288, 8192], P('ctx', 'head')
- query_grad: bfloat16 [12288, 8192], P('ctx', 'head')
- key_grad: float32 [12288, 1024], P('ctx', 'head')
- value_grad: float32 [12288, 1024], P('ctx', 'head')
The draws below stay inside these ranges and needn't reach their ends.
Inputs may be any that keep to these rules, and one draw needn't show every extreme that they name: Query and key entries lie within the range; in some draws a few queries are close to multiples of visible keys. doc_start[0] = 0; for i > 0 either doc_start[i] = i (a document begins) or doc_start[i] = doc_start[i - 1]. Documents may cross device boundaries. The last token begins a document of its own.
All inputs are finite; a program needn't handle non-finite values.
Results may differ from the reference program's by a relative error of at most 0.019.
Values may be sent and summed in bfloat16 or wider, within the bound.
A program may use at most 32 MiB of HBM per device.

```python
import math
import jax
import jax.numpy as jnp
from jax import lax

HEAD_DIM = 128
QUERY_HEADS = 64
KV_HEADS = 8
WINDOW = 1024
TOKENS = 12288


def query_key_pair(key):
    base_key = jax.random.fold_in(key, 7331)
    first, second = jax.random.split(base_key, 2)
    per_group = QUERY_HEADS // KV_HEADS
    query_draw = jax.random.normal(first, (TOKENS, KV_HEADS, per_group, HEAD_DIM), jnp.float32)
    key_draw = jax.random.normal(second, (TOKENS, KV_HEADS, HEAD_DIM), jnp.float32)
    query_draw = jnp.clip(query_draw, -6.0, 6.0)
    key_draw = jnp.clip(key_draw, -6.0, 6.0)
    query_draw = jnp.clip(query_draw, -24.0, 24.0)
    key_draw = jnp.clip(key_draw, -24.0, 24.0)
    return (query_draw.reshape(TOKENS, QUERY_HEADS * HEAD_DIM), key_draw.reshape(TOKENS, KV_HEADS * HEAD_DIM))


def draw_queries(key, part):
    return query_key_pair(key)[0].astype(jnp.bfloat16)


def draw_keys(key, part):
    return query_key_pair(key)[1].astype(jnp.bfloat16)


def draw_doc_start(key, part):
    ticket = jax.random.randint(jax.random.fold_in(key, 4242), (TOKENS,), 0, 2 * WINDOW)
    forced = jax.random.randint(jax.random.fold_in(key, 4343), (), TOKENS // 4, 3 * TOKENS // 4)
    position = jnp.arange(TOKENS, dtype=jnp.int32)
    begins = (ticket < 1) | (position == 0) | (position == TOKENS - 1) | (position == forced)
    marked = jnp.where(begins, position, 0).astype(jnp.int32)
    return lax.cummax(marked, axis=0).astype(jnp.int32)


def level_of(own_key, extent, pieces, low, top_value):
    def one(axis_at, blocks):
        heights = jax.random.uniform(jax.random.fold_in(jax.random.fold_in(own_key, 6), axis_at), (blocks,), jnp.float32, low / len(pieces), top_value / len(pieces))
        return jnp.repeat(jnp.exp(heights), extent[axis_at] // blocks).reshape((-1,) + (1,) * (len(extent) - axis_at - 1))

    factor_of = one(*pieces[0])
    for cut in pieces[1:]:
        factor_of = factor_of * one(*cut)
    return factor_of


def scatter_about(key, dims, deviation, most, shards=(), kind=jnp.bfloat16):
    result = deviation * jax.random.normal(key, dims, jnp.float32)
    if shards:
        result = result * level_of(key, dims, shards, -0.22, 0.18)
    return jnp.clip(result, -most, most).astype(kind)


def setup_inputs(seed: int = 0) -> dict:
    streams_of = jax.random.split(jax.random.key(seed), 6)
    queries = draw_queries(jax.random.fold_in(streams_of[5], 71), 0)
    keys = draw_keys(jax.random.fold_in(streams_of[5], 71), 0)
    values = scatter_about(streams_of[2], (TOKENS, KV_HEADS * HEAD_DIM), 1.0, 6.0, ((0, 24),))
    out_grad = scatter_about(streams_of[3], (TOKENS, QUERY_HEADS * HEAD_DIM), 1.0, 6.0, ((0, 24), (1, 32)))
    doc_start = draw_doc_start(jax.random.fold_in(streams_of[5], 71), 0)
    return {"queries": queries, "keys": keys, "values": values, "out_grad": out_grad, "doc_start": doc_start}


def reference(queries, keys, values, out_grad, doc_start):
    per_group = QUERY_HEADS // KV_HEADS
    block_rows = math.gcd(TOKENS, 512)
    score_scale = HEAD_DIM ** -0.5
    query_heads = queries.reshape(TOKENS, KV_HEADS, per_group, HEAD_DIM)
    grad_heads = out_grad.reshape(TOKENS, KV_HEADS, per_group, HEAD_DIM)
    padding = jnp.zeros((WINDOW, KV_HEADS, HEAD_DIM), keys.dtype)
    key_pad = jnp.concatenate([padding, keys.reshape(TOKENS, KV_HEADS, HEAD_DIM)], axis=0)
    value_pad = jnp.concatenate([padding, values.reshape(TOKENS, KV_HEADS, HEAD_DIM)], axis=0)

    def one_block(carry, row_start):
        key_acc, value_acc = carry
        query_block = lax.dynamic_slice_in_dim(query_heads, row_start, block_rows, 0).astype(jnp.float32)
        grad_block = lax.dynamic_slice_in_dim(grad_heads, row_start, block_rows, 0).astype(jnp.float32)
        key_block = lax.dynamic_slice_in_dim(key_pad, row_start, block_rows + WINDOW, 0).astype(jnp.float32)
        value_block = lax.dynamic_slice_in_dim(value_pad, row_start, block_rows + WINDOW, 0).astype(jnp.float32)
        starts = lax.dynamic_slice_in_dim(doc_start, row_start, block_rows, 0)
        query_pos = row_start + jnp.arange(block_rows, dtype=jnp.int32)
        key_pos = row_start - WINDOW + jnp.arange(block_rows + WINDOW, dtype=jnp.int32)
        visible = (key_pos[None, :] <= query_pos[:, None]) & (key_pos[None, :] > query_pos[:, None] - WINDOW) & (key_pos[None, :] >= starts[:, None])
        scores = jnp.einsum("qhgd,khd->hgqk", query_block, key_block) * score_scale
        masked = jnp.where(visible[None, None], scores, -1e30)
        row_max = jnp.max(masked, axis=-1, keepdims=True)
        weights = jnp.where(visible[None, None], jnp.exp(masked - row_max), 0.0)
        prob_full = weights / jnp.sum(weights, axis=-1, keepdims=True)
        prob_round = prob_full.astype(jnp.bfloat16).astype(jnp.float32)
        attended = jnp.einsum("hgqk,khd->qhgd", prob_round, value_block).astype(jnp.bfloat16)
        dprob = jnp.einsum("qhgd,khd->hgqk", grad_block, value_block)
        row_delta = jnp.transpose(jnp.sum(grad_block * attended.astype(jnp.float32), axis=-1), (1, 2, 0))
        dscore = (prob_full * (dprob - row_delta[..., None])).astype(jnp.bfloat16).astype(jnp.float32)
        q_grad = (jnp.einsum("hgqk,khd->qhgd", dscore, key_block) * score_scale).astype(jnp.bfloat16)
        key_part = jnp.einsum("hgqk,qhgd->khd", dscore, query_block) * score_scale
        value_part = jnp.einsum("hgqk,qhgd->khd", prob_round, grad_block)
        key_now = lax.dynamic_slice_in_dim(key_acc, row_start, block_rows + WINDOW, 0) + key_part
        value_now = lax.dynamic_slice_in_dim(value_acc, row_start, block_rows + WINDOW, 0) + value_part
        key_acc = lax.dynamic_update_slice_in_dim(key_acc, key_now, row_start, 0)
        value_acc = lax.dynamic_update_slice_in_dim(value_acc, value_now, row_start, 0)
        return (key_acc, value_acc), (attended, q_grad)

    block_starts = jnp.arange(TOKENS // block_rows, dtype=jnp.int32) * block_rows
    zero_acc = jnp.zeros((TOKENS + WINDOW, KV_HEADS, HEAD_DIM), jnp.float32)
    (key_acc, value_acc), (attended, q_grad) = lax.scan(one_block, (zero_acc, zero_acc), block_starts)
    attn_out = attended.reshape(TOKENS, QUERY_HEADS * HEAD_DIM)
    query_grad = q_grad.reshape(TOKENS, QUERY_HEADS * HEAD_DIM)
    key_grad = key_acc[WINDOW:].reshape(TOKENS, KV_HEADS * HEAD_DIM)
    value_grad = value_acc[WINDOW:].reshape(TOKENS, KV_HEADS * HEAD_DIM)
    return attn_out, query_grad, key_grad, value_grad
```

```python
import math

import jax
import jax.numpy as jnp
from jax import lax
from jax.experimental import pallas as pl
from jax.experimental.pallas import tpu as pltpu
from jax.sharding import PartitionSpec as P

D = 128
WINDOW = 1024
T = 512
H = 256
SCALE = D**-0.5
SCALE2 = SCALE * math.log2(math.e)
MESH = pl.DeviceIdType.MESH
f32, bf16 = jnp.float32, jnp.bfloat16

SEEN = {(0, 0): (0, H), (0, 1): (0, T), (1, 0): (0, T), (1, 1): (0, T), (2, 0): (0, T), (2, 1): (H, T)}


def dot(a, b, ca, cb):
    return lax.dot_general(a, b, (((ca,), (cb,)), ((), ())), preferred_element_type=f32)


def kernel(
    q_hbm, k_hbm, v_hbm, do_hbm, doc_ref,
    o_hbm, dq_hbm, dk_ref, dv_ref,
    q_in, do_in, kv, q2, do2, q_t, do_t, k_t, v_t,
    e_s, dp_s, m_s, l_s, dl_s, o_s,
    own, exch_out, exch_in, g1_out, g0_out, g1_in, g0_in,
    tot, y_out, y_in, o_vm, dq_vm,
    in_sem, out_sem, kv_send, kv_recv, relay_send, ex_send, ex_recv,
    g_send, g1_recv, g0_recv, y_send, y_recv,
):
    ctx = lax.axis_index("ctx")
    head = lax.axis_index("head")
    n_ctx = lax.axis_size("ctx")
    core = lax.rem(ctx, 2)
    even = core == 0
    group = head // 4
    member = lax.rem(head, 4)

    def at(step):
        return (ctx + step, head)

    def peer(j):
        return (ctx, group * 4 + lax.rem(member + j, 4))

    def remote(src, dst, ss, rs, dev):
        return pltpu.make_async_remote_copy(
            src_ref=src, dst_ref=dst, send_sem=ss, recv_sem=rs,
            device_id=dev, device_id_type=MESH,
        )

    cols = pl.ds(pl.multiple_of(group * D, D), D)
    loads = [
        pltpu.make_async_copy(k_hbm.at[:, cols], kv.at[0, 0], in_sem.at[0]),
        pltpu.make_async_copy(v_hbm.at[:, cols], kv.at[0, 1], in_sem.at[1]),
        pltpu.make_async_copy(q_hbm, q_in, in_sem.at[2]),
        pltpu.make_async_copy(do_hbm, do_in, in_sem.at[3]),
    ]
    for c in loads:
        c.start()

    has = {-2: ctx >= 2, -1: ctx >= 1, 1: ctx < n_ctx - 1, 2: ctx < n_ctx - 2}
    barrier = pltpu.get_barrier_semaphore()
    for step in (-1, 1, -2, 2):
        @pl.when(has[step])
        def _(step=step):
            pl.semaphore_signal(barrier, inc=1, device_id=at(step), device_id_type=MESH)
    for j in (1, 2, 3):
        pl.semaphore_signal(barrier, inc=1, device_id=peer(j), device_id_type=MESH)

    loads[0].wait()
    loads[1].wait()
    pl.semaphore_wait(barrier, 3 + sum(has[step].astype(jnp.int32) for step in (-1, 1, -2, 2)))

    def hop1(i):
        return remote(kv.at[0, i], kv.at[1, i], kv_send.at[0, i], kv_recv.at[1, i], at(1))

    def hop2(i):
        return remote(kv.at[0, i], kv.at[2, i], kv_send.at[1, i], kv_recv.at[2, i], at(2))

    def relay(i):
        return remote(kv.at[1, i], kv.at[2, i], relay_send.at[i], kv_recv.at[2, i], at(1))

    def recv2(i):
        return remote(kv.at[0, i], kv.at[2, i], kv_send.at[1, i], kv_recv.at[2, i], at(2))

    for i in (0, 1):
        @pl.when(has[1])
        def _(i=i):
            hop1(i).start()

        @pl.when(even & has[2])
        def _(i=i):
            hop2(i).start()

    @pl.when(ctx == 0)
    def _():
        kv[1] = jnp.zeros_like(kv[1])

    @pl.when(ctx <= 1)
    def _():
        kv[2] = jnp.zeros_like(kv[2])

    loads[2].wait()
    loads[3].wait()
    for half in range(2):
        for h in range(2):
            c = half * T + h * H
            a = q_in[half * H:(half + 1) * H, h * D:(h + 1) * D]
            q2[c:c + H, :] = a
            q_t[:, c:c + H] = a.T
            a = do_in[half * H:(half + 1) * H, h * D:(h + 1) * D]
            do2[c:c + H, :] = a
            do_t[:, c:c + H] = a.T

    doc = doc_ref[0:1, :] - ctx * T

    def forward(b):
        k_t[b] = kv[b, 0].T
        v_t[b] = kv[b, 1].T
        for half in range(2):
            lo_k, hi_k = SEEN[b, half]
            n = hi_k - lo_k
            c0 = half * T
            s = dot(kv[b, 0, lo_k:hi_k, :], q2[c0:c0 + T, :], 1, 1) * SCALE2
            key_pos = lax.broadcasted_iota(jnp.int32, (n, H), 0) + (lo_k - b * T)
            query_pos = lax.broadcasted_iota(jnp.int32, (1, H), 1) + half * H
            first = jnp.maximum(query_pos - (WINDOW - 1), doc[:, half * H:(half + 1) * H])
            visible = key_pos >= first
            if b == 0:
                visible = visible & (key_pos <= query_pos)
            visible = jnp.concatenate([visible, visible], axis=1)
            s = jnp.where(visible, s, -1e30)
            m = jnp.max(s, axis=0, keepdims=True)
            if b > 0:
                m_old = m_s[b - 1, 0:1, c0:c0 + T]
                m = jnp.maximum(m_old, m)
                alpha = jnp.exp2(m_old - m)
            e = jnp.exp2(s - m)
            dp = dot(kv[b, 1, lo_k:hi_k, :], do2[c0:c0 + T, :], 1, 1)
            l = jnp.sum(e, axis=0, keepdims=True)
            dl = jnp.sum(e * dp, axis=0, keepdims=True)
            if b > 0:
                l = l + alpha * l_s[0:1, c0:c0 + T]
                dl = dl + alpha * dl_s[0:1, c0:c0 + T]
            m_s[b, 0:1, c0:c0 + T] = m
            l_s[0:1, c0:c0 + T] = l
            dl_s[0:1, c0:c0 + T] = dl
            eb = e.astype(bf16)
            e_s[b, lo_k:hi_k, c0:c0 + T] = eb
            dp_s[b, lo_k:hi_k, c0:c0 + T] = dp
            o_s[b, :, c0:c0 + T] = dot(v_t[b, :, lo_k:hi_k], eb, 1, 0)

    forward(0)

    for i in (0, 1):
        @pl.when(has[-1])
        def _(i=i):
            hop1(i).wait_recv()

        @pl.when(even & has[-2])
        def _(i=i):
            relay(i).start()

    forward(1)

    for i in (0, 1):
        @pl.when(has[-2])
        def _(i=i):
            recv2(i).wait_recv()

    forward(2)

    l_inv = 1.0 / l_s[0:1, :]
    delta = dl_s[0:1, :] * l_inv
    m = m_s[2, 0:1, :]

    def coef(b):
        return jnp.exp2(m_s[b, 0:1, :] - m) * l_inv

    def assemble(b, parts):
        p0, p1 = parts
        if b == 0:
            return [(0, H, p0 + p1[:H]), (H, T, p1[H:])]
        if b == 1:
            return [(0, T, p0 + p1)]
        return [(0, H, p0[:H]), (H, T, p0[H:] + p1)]

    def value_part(b):
        w = (do_t[...].astype(f32) * coef(b)).astype(bf16)
        parts = []
        for half in range(2):
            lo_k, hi_k = SEEN[b, half]
            c0 = half * T
            parts.append(dot(e_s[b, lo_k:hi_k, c0:c0 + T], w[:, c0:c0 + T], 1, 1))
        return assemble(b, parts)

    dq_acc = [None, None]

    def key_part(b):
        c_b = coef(b)
        w = (q_t[...].astype(f32) * (c_b * SCALE)).astype(bf16)
        parts = []
        for half in range(2):
            lo_k, hi_k = SEEN[b, half]
            c0 = half * T
            ds = e_s[b, lo_k:hi_k, c0:c0 + T].astype(f32)
            ds = (ds * (dp_s[b, lo_k:hi_k, c0:c0 + T] - delta[:, c0:c0 + T])).astype(bf16)
            parts.append(dot(ds, w[:, c0:c0 + T], 1, 1))
            dq = dot(k_t[b, :, lo_k:hi_k], ds, 1, 0) * (c_b[:, c0:c0 + T] * SCALE)
            dq_acc[half] = dq if dq_acc[half] is None else dq_acc[half] + dq
        return assemble(b, parts)

    def exch(i, step):
        return remote(exch_out, exch_in, ex_send, ex_recv, at(step))

    def send_g1(i):
        return remote(g1_out.at[i], g1_in.at[i], g_send.at[0, i], g1_recv.at[i], at(-1))

    def send_g0(i):
        return remote(g0_out.at[i], g0_in.at[i], g_send.at[1, i], g0_recv.at[i], at(-2))

    for a, z, p in value_part(2):
        g0_out[1, a:z, :] = p.astype(bf16)

    @pl.when(jnp.logical_not(even) & has[-2])
    def _():
        exch_out[...] = g0_out[1]
        exch(1, -1).start()

    @pl.when(even & has[-2])
    def _():
        send_g0(1).start()

    for a, z, p in value_part(1):
        own[1, a:z, :] = p

    @pl.when(jnp.logical_not(even))
    def _():
        g1_out[1] = own[1].astype(bf16)
        send_g1(1).start()

    for a, z, p in key_part(2):
        tot[0, a:z, :] = p

    @pl.when(even & has[-2])
    def _():
        g0_out[0] = tot[0].astype(bf16)
        send_g0(0).start()
        exch(1, 1).wait_recv()
        g1_out[1] = (own[1] + exch_in[...].astype(f32)).astype(bf16)
        send_g1(1).start()

    for a, z, p in key_part(1):
        own[0, a:z, :] = p

    @pl.when(jnp.logical_not(even))
    def _():
        g1_out[0] = own[0].astype(bf16)
        send_g1(0).start()

    @pl.when(even & has[-2])
    def _():
        exch_out[...] = own[0].astype(bf16)
        exch(0, 1).start()

    for a, z, p in value_part(0):
        own[1, a:z, :] = p

    @pl.when(jnp.logical_not(even) & has[-2])
    def _():
        exch(0, -1).wait_recv()
        g0_out[0] = (tot[0] + exch_in[...].astype(f32)).astype(bf16)
        send_g0(0).start()

    for a, z, p in key_part(0):
        own[0, a:z, :] = p

    for half in range(2):
        c0 = half * T
        o = None
        for b in range(3):
            part = o_s[b, :, c0:c0 + T] * coef(b)[:, c0:c0 + T]
            o = part if o is None else o + part
        for h in range(2):
            rows, lanes = slice(half * H, (half + 1) * H), slice(h * D, (h + 1) * D)
            o_vm[rows, lanes] = o[:, h * H:(h + 1) * H].T.astype(bf16)
            dq_vm[rows, lanes] = dq_acc[half][:, h * H:(h + 1) * H].T.astype(bf16)
    stores = [
        pltpu.make_async_copy(o_vm, o_hbm, out_sem.at[0]),
        pltpu.make_async_copy(dq_vm, dq_hbm, out_sem.at[1]),
    ]
    for c in stores:
        c.start()

    def y_copy(i, j):
        to = lax.rem(member + j, 4)
        return remote(
            y_out.at[i, pl.ds(pl.multiple_of(to * 32, 32), 32), :], y_in.at[i, j - 1],
            y_send.at[i, j - 1], y_recv.at[i, j - 1], peer(j),
        )

    for i in (1, 0):
        tot[i] = own[i]

        @pl.when(even)
        def _(i=i):
            send_g1(i).wait_recv()
            tot[i] += g1_in[i].astype(f32)

        @pl.when(even & has[2])
        def _(i=i):
            send_g0(i).wait_recv()
            tot[i] += g0_in[i].astype(f32)

        @pl.when(jnp.logical_not(even) & has[1])
        def _(i=i):
            if i == 1:
                send_g1(1).wait_recv()
                tot[1] += g1_in[1].astype(f32)
            else:
                send_g0(0).wait_recv()
                tot[0] += g0_in[0].astype(f32)

        tt = tot[i].T
        own[i] = jnp.concatenate([tt[:, 0:D], tt[:, D:2 * D], tt[:, 2 * D:3 * D], tt[:, 3 * D:]], axis=0)
        y_out[i] = tt.astype(bf16)
        for j in (1, 2, 3):
            y_copy(i, j).start()

    for i, out in ((1, dv_ref), (0, dk_ref)):
        mine = pl.multiple_of(member * 32, 32)
        acc = [own[i, pl.ds(mine + D * c, 32), :] for c in range(4)]
        acc = jnp.concatenate(acc, axis=1)
        for j in (1, 2, 3):
            y_copy(i, j).wait_recv()
            acc = acc + y_in[i, j - 1].astype(f32)
        out[...] = acc

    for i in (0, 1):
        @pl.when(has[1])
        def _(i=i):
            hop1(i).wait_send()

        @pl.when(even & has[2])
        def _(i=i):
            hop2(i).wait_send()

        @pl.when(even & has[-2])
        def _(i=i):
            relay(i).wait_send()
            send_g0(i).wait_send()

        @pl.when(jnp.logical_not(even))
        def _(i=i):
            send_g1(i).wait_send()
        for j in (1, 2, 3):
            y_copy(i, j).wait_send()

    @pl.when(even & has[-2])
    def _():
        send_g1(1).wait_send()
        exch(0, 1).wait_send()

    @pl.when(jnp.logical_not(even) & has[-2])
    def _():
        send_g0(0).wait_send()
        exch(1, -1).wait_send()
    for c in stores:
        c.wait()


def body(queries, keys, values, out_grad, doc_start):
    hbm = pl.BlockSpec(memory_space=pl.ANY)
    vmem = pl.BlockSpec(memory_space=pltpu.VMEM)
    V, DMA = pltpu.VMEM, pltpu.SemaphoreType.DMA
    S = jax.ShapeDtypeStruct
    o, dq, dk, dv = pl.pallas_call(
        kernel,
        out_shape=(S((T, 2 * D), bf16), S((T, 2 * D), bf16), S((32, T), f32), S((32, T), f32)),
        in_specs=[hbm, hbm, hbm, hbm, vmem],
        out_specs=(hbm, hbm, vmem, vmem),
        scratch_shapes=[
            V((T, 2 * D), bf16), V((T, 2 * D), bf16), V((3, 2, T, D), bf16),
            V((2 * T, D), bf16), V((2 * T, D), bf16), V((D, 2 * T), bf16), V((D, 2 * T), bf16),
            V((3, D, T), bf16), V((3, D, T), bf16),
            V((3, T, 2 * T), bf16), V((3, T, 2 * T), f32),
            V((3, 8, 2 * T), f32), V((8, 2 * T), f32), V((8, 2 * T), f32), V((3, D, 2 * T), f32),
            V((2, T, D), f32), V((T, D), bf16), V((T, D), bf16),
            V((2, T, D), bf16), V((2, T, D), bf16), V((2, T, D), bf16), V((2, T, D), bf16),
            V((2, T, D), f32), V((2, D, T), bf16), V((2, 3, 32, T), bf16),
            V((T, 2 * D), bf16), V((T, 2 * D), bf16),
            DMA((4,)), DMA((2,)), DMA((2, 2)), DMA((3, 2)), DMA((2,)), DMA(()), DMA(()),
            DMA((2, 2)), DMA((2,)), DMA((2,)), DMA((2, 3)), DMA((2, 3)),
        ],
        compiler_params=pltpu.CompilerParams(
            collective_id=0, has_side_effects=True, vmem_limit_bytes=56 * 2**20
        ),
    )(queries, keys, values, out_grad, doc_start.reshape(1, T))
    return o, dq, dk.T, dv.T


def solution(mesh):
    placed = (P("ctx", "head"), P("ctx", None), P("ctx", None), P("ctx", "head"), P("ctx"))
    return jax.shard_map(
        body,
        mesh=mesh,
        in_specs=placed,
        out_specs=(P("ctx", "head"),) * 4,
        check_vma=False,
    )
```

```python
import math

import jax
import jax.numpy as jnp
from jax import lax
from jax.experimental import pallas as pl
from jax.experimental.pallas import tpu as pltpu
from jax.sharding import PartitionSpec as P

D = 128
WINDOW = 1024
T = 512
H = 256
SCALE = D**-0.5
SCALE2 = SCALE * math.log2(math.e)
MESH = pl.DeviceIdType.MESH
f32, bf16 = jnp.float32, jnp.bfloat16

SEEN = {(0, 0): (0, H), (0, 1): (0, T), (1, 0): (0, T), (1, 1): (0, T), (2, 0): (0, T), (2, 1): (H, T)}


def dot(a, b, ca, cb):
    return lax.dot_general(a, b, (((ca,), (cb,)), ((), ())), preferred_element_type=f32)


def kernel(
    q_hbm, k_hbm, v_hbm, do_hbm, doc_hbm,
    o_vm, dq_vm, dk_ref, dv_ref,
    q_in, do_in, kv, q2, do2, q_t, do_t, k_t, v_t,
    e_s, dp_s, m_s, l_s, dl_s, o_s, doc_ref, o_acc, dq_s,
    own, exch_out, exch_in, g1_out, g0_out, g1_in, g0_in,
    tot, y_out, y_in,
    in_sem, kv_send, kv_recv, relay_send, ex_send, ex_recv,
    g_send, g1_recv, g0_recv, y_send, y_recv,
):
    ctx = lax.axis_index("ctx")
    head = lax.axis_index("head")
    n_ctx = lax.axis_size("ctx")
    core = lax.rem(ctx, 2)
    even = core == 0
    group = head // 4
    member = lax.rem(head, 4)

    def at(step):
        return (ctx + step, head)

    def peer(j):
        return (ctx, group * 4 + lax.rem(member + j, 4))

    def remote(src, dst, ss, rs, dev):
        return pltpu.make_async_remote_copy(
            src_ref=src, dst_ref=dst, send_sem=ss, recv_sem=rs,
            device_id=dev, device_id_type=MESH,
        )

    cols = pl.ds(pl.multiple_of(group * D, D), D)
    loads = [
        pltpu.make_async_copy(k_hbm.at[:, cols], kv.at[0, 0], in_sem.at[0]),
        pltpu.make_async_copy(v_hbm.at[:, cols], kv.at[0, 1], in_sem.at[1]),
        pltpu.make_async_copy(q_hbm, q_in, in_sem.at[2]),
        pltpu.make_async_copy(do_hbm, do_in, in_sem.at[3]),
        pltpu.make_async_copy(doc_hbm, doc_ref, in_sem.at[4]),
    ]
    for c in loads:
        c.start()

    has = {-2: ctx >= 2, -1: ctx >= 1, 1: ctx < n_ctx - 1, 2: ctx < n_ctx - 2}
    barrier = pltpu.get_barrier_semaphore()
    for j in (1, 2, 3):
        pl.semaphore_signal(barrier, inc=1, device_id=peer(j), device_id_type=MESH)

    @pl.when(has[-1])
    def _():
        pl.semaphore_signal(barrier, inc=1, device_id=at(-1), device_id_type=MESH)

    @pl.when(even & has[-2])
    def _():
        pl.semaphore_signal(barrier, inc=1, device_id=at(-2), device_id_type=MESH)

    dq_s[...] = jnp.zeros_like(dq_s)
    o_acc[...] = jnp.zeros_like(o_acc)
    loads[0].wait()
    loads[1].wait()
    receivers = has[1].astype(jnp.int32) + (even & has[2]).astype(jnp.int32)
    pl.semaphore_wait(barrier, 3 + receivers)

    def hop1(i):
        return remote(kv.at[0, i], kv.at[1, i], kv_send.at[0, i], kv_recv.at[1, i], at(1))

    def hop2(i):
        return remote(kv.at[0, i], kv.at[2, i], kv_send.at[1, i], kv_recv.at[2, i], at(2))

    def relay(i):
        return remote(kv.at[1, i], kv.at[2, i], relay_send.at[i], kv_recv.at[2, i], at(1))

    def recv2(i):
        return remote(kv.at[0, i], kv.at[2, i], kv_send.at[1, i], kv_recv.at[2, i], at(2))

    for i in (0, 1):
        @pl.when(has[1])
        def _(i=i):
            hop1(i).start()

        @pl.when(even & has[2])
        def _(i=i):
            hop2(i).start()

    loads[2].wait()
    loads[3].wait()
    loads[4].wait()
    for half in range(2):
        for h in range(2):
            c = half * T + h * H
            a = q_in[half * H:(half + 1) * H, h * D:(h + 1) * D]
            q2[c:c + H, :] = a
            q_t[:, c:c + H] = a.T
            a = do_in[half * H:(half + 1) * H, h * D:(h + 1) * D]
            do2[c:c + H, :] = a
            do_t[:, c:c + H] = a.T

    doc = doc_ref[0:1, :] - ctx * T

    def forward(b):
        k_t[b] = kv[b, 0].T
        v_t[b] = kv[b, 1].T
        for half in range(2):
            lo_k, hi_k = SEEN[b, half]
            n = hi_k - lo_k
            c0 = half * T
            s = dot(kv[b, 0, lo_k:hi_k, :], q2[c0:c0 + T, :], 1, 1) * SCALE2
            key_pos = lax.broadcasted_iota(jnp.int32, (n, H), 0) + (lo_k - b * T)
            query_pos = lax.broadcasted_iota(jnp.int32, (1, H), 1) + half * H
            first = jnp.maximum(query_pos - (WINDOW - 1), doc[:, half * H:(half + 1) * H])
            visible = key_pos >= first
            if b == 0:
                visible = visible & (key_pos <= query_pos)
            visible = jnp.concatenate([visible, visible], axis=1)
            s = jnp.where(visible, s, -1e30)
            m = jnp.max(s, axis=0, keepdims=True)
            if b > 0:
                m_old = m_s[3, 0:1, c0:c0 + T]
                m = jnp.maximum(m_old, m)
                alpha = jnp.exp2(m_old - m)
            e = jnp.exp2(s - m)
            dp = dot(kv[b, 1, lo_k:hi_k, :], do2[c0:c0 + T, :], 1, 1)
            l = jnp.sum(e, axis=0, keepdims=True)
            dl = jnp.sum(e * dp, axis=0, keepdims=True)
            if b > 0:
                l = l + alpha * l_s[0:1, c0:c0 + T]
                dl = dl + alpha * dl_s[0:1, c0:c0 + T]
            m_s[b, 0:1, c0:c0 + T] = m
            m_s[3, 0:1, c0:c0 + T] = m
            l_s[0:1, c0:c0 + T] = l
            dl_s[0:1, c0:c0 + T] = dl
            eb = e.astype(bf16)
            e_s[b, lo_k:hi_k, c0:c0 + T] = eb
            dp_s[b, lo_k:hi_k, c0:c0 + T] = dp
            o_s[b, :, c0:c0 + T] = dot(v_t[b, :, lo_k:hi_k], eb, 1, 0)

    forward(0)

    @pl.when(has[-1])
    def _():
        for i in (0, 1):
            hop1(i).wait_recv()

            @pl.when(even)
            def _(i=i):
                relay(i).start()
        forward(1)

    @pl.when(has[-2])
    def _():
        for i in (0, 1):
            recv2(i).wait_recv()
        forward(2)

    l_inv = 1.0 / l_s[0:1, :]
    delta = dl_s[0:1, :] * l_inv
    m = m_s[3, 0:1, :]

    def coef(b):
        return jnp.exp2(m_s[b, 0:1, :] - m) * l_inv

    def assemble(b, parts):
        p0, p1 = parts
        if b == 0:
            return [(0, H, p0 + p1[:H]), (H, T, p1[H:])]
        if b == 1:
            return [(0, T, p0 + p1)]
        return [(0, H, p0[:H]), (H, T, p0[H:] + p1)]

    def value_part(b):
        w = (do_t[...].astype(f32) * coef(b)).astype(bf16)
        parts = []
        for half in range(2):
            lo_k, hi_k = SEEN[b, half]
            c0 = half * T
            parts.append(dot(e_s[b, lo_k:hi_k, c0:c0 + T], w[:, c0:c0 + T], 1, 1))
        return assemble(b, parts)

    def key_part(b):
        c_b = coef(b)
        w = (q_t[...].astype(f32) * (c_b * SCALE)).astype(bf16)
        parts = []
        for half in range(2):
            lo_k, hi_k = SEEN[b, half]
            c0 = half * T
            ds = e_s[b, lo_k:hi_k, c0:c0 + T].astype(f32)
            ds = (ds * (dp_s[b, lo_k:hi_k, c0:c0 + T] - delta[:, c0:c0 + T])).astype(bf16)
            parts.append(dot(ds, w[:, c0:c0 + T], 1, 1))
            dq = dot(k_t[b, :, lo_k:hi_k], ds, 1, 0) * (c_b[:, c0:c0 + T] * SCALE)
            dq_s[:, c0:c0 + T] += dq
            o_acc[:, c0:c0 + T] += o_s[b, :, c0:c0 + T] * c_b[:, c0:c0 + T]
        return assemble(b, parts)

    def exch(i, step):
        return remote(exch_out, exch_in, ex_send, ex_recv, at(step))

    def send_g1(i):
        return remote(g1_out.at[i], g1_in.at[i], g_send.at[0, i], g1_recv.at[i], at(-1))

    def send_g0(i):
        return remote(g0_out.at[i], g0_in.at[i], g_send.at[1, i], g0_recv.at[i], at(-2))

    @pl.when(has[-2])
    def _():
        for a, z, p in value_part(2):
            g0_out[1, a:z, :] = p.astype(bf16)

        @pl.when(even)
        def _():
            send_g0(1).start()

        @pl.when(jnp.logical_not(even))
        def _():
            exch_out[...] = g0_out[1]
            exch(1, -1).start()

    @pl.when(has[-1])
    def _():
        for a, z, p in value_part(1):
            own[1, a:z, :] = p

        @pl.when(jnp.logical_not(even))
        def _():
            g1_out[1] = own[1].astype(bf16)
            send_g1(1).start()

    @pl.when(has[-2])
    def _():
        for a, z, p in key_part(2):
            tot[0, a:z, :] = p

        @pl.when(even)
        def _():
            g0_out[0] = tot[0].astype(bf16)
            send_g0(0).start()
            exch(1, 1).wait_recv()
            g1_out[1] = (own[1] + exch_in[...].astype(f32)).astype(bf16)
            send_g1(1).start()

    @pl.when(has[-1])
    def _():
        for a, z, p in key_part(1):
            own[0, a:z, :] = p

        @pl.when(even)
        def _():
            exch_out[...] = own[0].astype(bf16)
            exch(0, 1).start()

        @pl.when(jnp.logical_not(even))
        def _():
            g1_out[0] = own[0].astype(bf16)
            send_g1(0).start()

    for a, z, p in value_part(0):
        own[1, a:z, :] = p

    @pl.when(jnp.logical_not(even) & has[-2])
    def _():
        exch(0, -1).wait_recv()
        g0_out[0] = (tot[0] + exch_in[...].astype(f32)).astype(bf16)
        send_g0(0).start()

    for a, z, p in key_part(0):
        own[0, a:z, :] = p

    for half in range(2):
        for h in range(2):
            c = half * T + h * H
            rows, lanes = slice(half * H, (half + 1) * H), slice(h * D, (h + 1) * D)
            o_vm[rows, lanes] = o_acc[:, c:c + H].T.astype(bf16)
            dq_vm[rows, lanes] = dq_s[:, c:c + H].T.astype(bf16)

    def y_copy(i, j):
        to = lax.rem(member + j, 4)
        return remote(
            y_out.at[i, pl.ds(pl.multiple_of(to * 32, 32), 32), :], y_in.at[i, j - 1],
            y_send.at[i, j - 1], y_recv.at[i, j - 1], peer(j),
        )

    for i in (1, 0):
        tot[i] = own[i]

        @pl.when(even)
        def _(i=i):
            send_g1(i).wait_recv()
            tot[i] += g1_in[i].astype(f32)

        @pl.when(even & has[2])
        def _(i=i):
            send_g0(i).wait_recv()
            tot[i] += g0_in[i].astype(f32)

        @pl.when(jnp.logical_not(even) & has[1])
        def _(i=i):
            if i == 1:
                send_g1(1).wait_recv()
                tot[1] += g1_in[1].astype(f32)
            else:
                send_g0(0).wait_recv()
                tot[0] += g0_in[0].astype(f32)

        tt = tot[i].T
        own[i] = jnp.concatenate([tt[:, 0:D], tt[:, D:2 * D], tt[:, 2 * D:3 * D], tt[:, 3 * D:]], axis=0)
        y_out[i] = tt.astype(bf16)
        for j in (1, 2, 3):
            y_copy(i, j).start()

    for i, out in ((1, dv_ref), (0, dk_ref)):
        mine = pl.multiple_of(member * 32, 32)
        acc = [own[i, pl.ds(mine + D * c, 32), :] for c in range(4)]
        acc = jnp.concatenate(acc, axis=1)
        for j in (1, 2, 3):
            y_copy(i, j).wait_recv()
            acc = acc + y_in[i, j - 1].astype(f32)
        out[...] = acc

    for i in (0, 1):
        @pl.when(has[1])
        def _(i=i):
            hop1(i).wait_send()

        @pl.when(even & has[2])
        def _(i=i):
            hop2(i).wait_send()

        @pl.when(even & has[-2])
        def _(i=i):
            relay(i).wait_send()
            send_g0(i).wait_send()

        @pl.when(jnp.logical_not(even))
        def _(i=i):
            send_g1(i).wait_send()
        for j in (1, 2, 3):
            y_copy(i, j).wait_send()

    @pl.when(even & has[-2])
    def _():
        send_g1(1).wait_send()
        exch(0, 1).wait_send()

    @pl.when(jnp.logical_not(even) & has[-2])
    def _():
        send_g0(0).wait_send()
        exch(1, -1).wait_send()


def place(o, dq, dk, dv, o_out, dq_out, dk_out, dv_out, sem):
    pairs = ((o, o_out), (dq, dq_out), (dk, dk_out), (dv, dv_out))
    copies = [pltpu.make_async_copy(a, b, sem.at[i]) for i, (a, b) in enumerate(pairs)]
    for c in copies:
        c.start()
    for c in copies:
        c.wait()


def body(queries, keys, values, out_grad, doc_start):
    hbm = pl.BlockSpec(memory_space=pltpu.HBM)
    vmem = pl.BlockSpec(memory_space=pltpu.VMEM)
    V, DMA = pltpu.VMEM, pltpu.SemaphoreType.DMA
    S = jax.ShapeDtypeStruct
    o, dq, dk, dv = pl.pallas_call(
        kernel,
        out_shape=(S((T, 2 * D), bf16), S((T, 2 * D), bf16), S((32, T), f32), S((32, T), f32)),
        in_specs=[hbm] * 5,
        out_specs=(vmem,)*4,
        scratch_shapes=[
            V((T, 2 * D), bf16), V((T, 2 * D), bf16), V((3, 2, T, D), bf16),
            V((2 * T, D), bf16), V((2 * T, D), bf16), V((D, 2 * T), bf16), V((D, 2 * T), bf16),
            V((3, D, T), bf16), V((3, D, T), bf16),
            V((3, T, 2 * T), bf16), V((3, T, 2 * T), f32),
            V((4, 8, 2 * T), f32), V((8, 2 * T), f32), V((8, 2 * T), f32), V((3, D, 2 * T), f32),
            V((1, T), jnp.int32), V((D, 2 * T), f32), V((D, 2 * T), f32),
            V((2, T, D), f32), V((T, D), bf16), V((T, D), bf16),
            V((2, T, D), bf16), V((2, T, D), bf16), V((2, T, D), bf16), V((2, T, D), bf16),
            V((2, T, D), f32), V((2, D, T), bf16), V((2, 3, 32, T), bf16),
            DMA((5,)), DMA((2, 2)), DMA((3, 2)), DMA((2,)), DMA(()), DMA(()),
            DMA((2, 2)), DMA((2,)), DMA((2,)), DMA((2, 3)), DMA((2, 3)),
        ],
        compiler_params=pltpu.CompilerParams(
            collective_id=0, has_side_effects=True, vmem_limit_bytes=int(53.25 * 2**20)
        ),
    )(queries, keys, values, out_grad, doc_start.reshape(1, T))
    o, dq, dk, dv = pl.pallas_call(
        place,
        out_shape=(S((T, 2 * D), bf16), S((T, 2 * D), bf16), S((32, T), f32), S((32, T), f32)),
        in_specs=[vmem] * 4,
        out_specs=(hbm,) * 4,
        scratch_shapes=[DMA((4,))],
        compiler_params=pltpu.CompilerParams(vmem_limit_bytes=4 * 2**20),
    )(o, dq, dk, dv)
    return o, dq, dk.T, dv.T


def solution(mesh):
    placed = (P("ctx", "head"), P("ctx", None), P("ctx", None), P("ctx", "head"), P("ctx"))
    return jax.shard_map(
        body,
        mesh=mesh,
        in_specs=placed,
        out_specs=(P("ctx", "head"),) * 4,
        check_vma=False,
    )
```

```python
import math

import jax
import jax.numpy as jnp
from jax import lax
from jax.experimental import pallas as pl
from jax.experimental.pallas import tpu as pltpu
from jax.sharding import PartitionSpec as P

D = 128
WINDOW = 1024
T = 512
H = 256
SCALE = D**-0.5
SCALE2 = SCALE * math.log2(math.e)
MESH = pl.DeviceIdType.MESH
f32, bf16 = jnp.float32, jnp.bfloat16

SEEN = {(0, 0): (0, H), (0, 1): (0, T), (1, 0): (0, T), (1, 1): (0, T), (2, 0): (0, T), (2, 1): (H, T)}


def dot(a, b, ca, cb):
    return lax.dot_general(a, b, (((ca,), (cb,)), ((), ())), preferred_element_type=f32)


PIECES = ((1, 0, T), (0, 0, H), (0, H, T))


def kernel(
    q_hbm, k_hbm, v_hbm, do_hbm, doc_hbm,
    o_vm, dq_vm, dk_ref, dv_ref,
    q_in, do_in, doc_ref, kv, q2, do2, q_t, do_t,
    e_s, dp_s, ds_s, m_s, l_s, dl_s, c_s, delta_s, o_acc, dq_s,
    own, part, exch_out, exch_in, g1_out, g0_out, g1_in, g0_in, y_out, y_in,
    in_sem, kv_send, kv_recv, relay_send, ex_send, ex_recv,
    g1_send, g1_recv, g0_send, g0_recv, y_send, y_recv,
):
    ctx = lax.axis_index("ctx")
    head = lax.axis_index("head")
    n_ctx = lax.axis_size("ctx")
    core = lax.rem(ctx, 2)
    even = core == 0
    odd = core == 1
    group = head // 4
    member = lax.rem(head, 4)

    def at(step):
        return (ctx + step, head)

    def peer(j):
        return (ctx, group * 4 + lax.rem(member + j, 4))

    def remote(src, dst, ss, rs, dev):
        return pltpu.make_async_remote_copy(
            src_ref=src, dst_ref=dst, send_sem=ss, recv_sem=rs,
            device_id=dev, device_id_type=MESH,
        )

    cols = pl.ds(pl.multiple_of(group * D, D), D)
    loads = [
        pltpu.make_async_copy(k_hbm.at[:, cols], kv.at[0, 0], in_sem.at[0]),
        pltpu.make_async_copy(v_hbm.at[:, cols], kv.at[0, 1], in_sem.at[1]),
        pltpu.make_async_copy(q_hbm, q_in, in_sem.at[2]),
        pltpu.make_async_copy(do_hbm, do_in, in_sem.at[3]),
        pltpu.make_async_copy(doc_hbm, doc_ref, in_sem.at[4]),
    ]
    for c in loads:
        c.start()

    has = {-2: ctx >= 2, -1: ctx >= 1, 1: ctx < n_ctx - 1, 2: ctx < n_ctx - 2}
    barrier = pltpu.get_barrier_semaphore()
    for j in (1, 2, 3):
        pl.semaphore_signal(barrier, inc=1, device_id=peer(j), device_id_type=MESH)

    @pl.when(has[-1])
    def _():
        pl.semaphore_signal(barrier, inc=1, device_id=at(-1), device_id_type=MESH)

    @pl.when(even & has[-2])
    def _():
        pl.semaphore_signal(barrier, inc=1, device_id=at(-2), device_id_type=MESH)

    loads[0].wait()
    loads[1].wait()
    receivers = has[1].astype(jnp.int32) + (even & has[2]).astype(jnp.int32)
    pl.semaphore_wait(barrier, 3 + receivers)

    def hop1(i):
        return remote(kv.at[0, i], kv.at[1, i], kv_send.at[0, i], kv_recv.at[1, i], at(1))

    def hop2(i):
        return remote(kv.at[0, i], kv.at[2, i], kv_send.at[1, i], kv_recv.at[2, i], at(2))

    def relay(i):
        return remote(kv.at[1, i], kv.at[2, i], relay_send.at[i], kv_recv.at[2, i], at(1))

    def recv2(i):
        return remote(kv.at[0, i], kv.at[2, i], kv_send.at[1, i], kv_recv.at[2, i], at(2))

    for i in (0, 1):
        @pl.when(has[1])
        def _(i=i):
            hop1(i).start()

        @pl.when(even & has[2])
        def _(i=i):
            hop2(i).start()

    loads[2].wait()
    loads[3].wait()
    loads[4].wait()
    for half in range(2):
        for h in range(2):
            c = half * T + h * H
            a = q_in[half * H:(half + 1) * H, h * D:(h + 1) * D]
            q2[c:c + H, :] = a
            q_t[:, c:c + H] = a.T
            a = do_in[half * H:(half + 1) * H, h * D:(h + 1) * D]
            do2[c:c + H, :] = a
            do_t[:, c:c + H] = a.T

    doc = doc_ref[0:1, :] - ctx * T

    def score(b):
        for half in range(2):
            lo_k, hi_k = SEEN[b, half]
            n = hi_k - lo_k
            c0 = half * T
            s = dot(kv[b, 0, lo_k:hi_k, :], q2[c0:c0 + T, :], 1, 1) * SCALE2
            key_pos = lax.broadcasted_iota(jnp.int32, (n, H), 0) + (lo_k - b * T)
            query_pos = lax.broadcasted_iota(jnp.int32, (1, H), 1) + half * H
            first = jnp.maximum(query_pos - (WINDOW - 1), doc[:, half * H:(half + 1) * H])
            visible = key_pos >= first
            if b == 0:
                visible = visible & (key_pos <= query_pos)
            visible = jnp.concatenate([visible, visible], axis=1)
            s = jnp.where(visible, s, -1e30)
            m = jnp.max(s, axis=0, keepdims=True)
            if b > 0:
                m_old = m_s[3, 0:1, c0:c0 + T]
                m = jnp.maximum(m_old, m)
            e = jnp.exp2(s - m)
            l = jnp.sum(e, axis=0, keepdims=True)
            if b > 0:
                l = l + jnp.exp2(m_old - m) * l_s[0:1, c0:c0 + T]
            m_s[b, 0:1, c0:c0 + T] = m
            m_s[3, 0:1, c0:c0 + T] = m
            l_s[0:1, c0:c0 + T] = l
            e_s[b, lo_k:hi_k, c0:c0 + T] = e.astype(bf16)

    def dprob(b):
        for half in range(2):
            lo_k, hi_k = SEEN[b, half]
            c0 = half * T
            dp = dot(kv[b, 1, lo_k:hi_k, :], do2[c0:c0 + T, :], 1, 1)
            dp_s[b, lo_k:hi_k, c0:c0 + T] = dp
            e = e_s[b, lo_k:hi_k, c0:c0 + T].astype(f32)
            dl = jnp.sum(e * dp, axis=0, keepdims=True)
            if b == 0:
                dl_s[0:1, c0:c0 + T] = dl
            else:
                delta_s[0:1, c0:c0 + T] += dl * c_s[b, 0:1, c0:c0 + T]

    def coef(b):
        c_s[b, 0:1, :] = jnp.exp2(m_s[b, 0:1, :] - m_s[3, 0:1, :]) / l_s[0:1, :]

    def assemble(b, p):
        if b == 0:
            return [(0, H, p[0] + p[1][:, :H]), (H, T, p[1][:, H:])]
        if b == 1:
            return [(0, T, p[0] + p[1])]
        return [(0, H, p[0][:, :H]), (H, T, p[0][:, H:] + p[1])]

    def value_part(b):
        w = (do_t[...].astype(f32) * c_s[b, 0:1, :]).astype(bf16)
        parts = []
        for half in range(2):
            lo_k, hi_k = SEEN[b, half]
            c0 = half * T
            parts.append(dot(w[:, c0:c0 + T], e_s[b, lo_k:hi_k, c0:c0 + T], 1, 1))
        return assemble(b, parts)

    def key_part(b):
        w = (q_t[...].astype(f32) * (c_s[b, 0:1, :] * SCALE)).astype(bf16)
        parts = []
        for half in range(2):
            lo_k, hi_k = SEEN[b, half]
            c0 = half * T
            ds = e_s[b, lo_k:hi_k, c0:c0 + T].astype(f32)
            ds = (ds * (dp_s[b, lo_k:hi_k, c0:c0 + T] - delta_s[0:1, c0:c0 + T])).astype(bf16)
            ds_s[b, lo_k:hi_k, c0:c0 + T] = ds
            parts.append(dot(w[:, c0:c0 + T], ds, 1, 1))
        return assemble(b, parts)

    def row_parts(b):
        k_t, v_t = kv[b, 0].T, kv[b, 1].T
        for half in range(2):
            lo_k, hi_k = SEEN[b, half]
            c0 = half * T
            c = c_s[b, 0:1, c0:c0 + T]
            o = dot(v_t[:, lo_k:hi_k], e_s[b, lo_k:hi_k, c0:c0 + T], 1, 0) * c
            dq = dot(k_t[:, lo_k:hi_k], ds_s[b, lo_k:hi_k, c0:c0 + T], 1, 0) * (c * SCALE)
            if b == 0:
                o_acc[:, c0:c0 + T] = o
                dq_s[:, c0:c0 + T] = dq
            else:
                o_acc[:, c0:c0 + T] += o
                dq_s[:, c0:c0 + T] += dq

    def piece(ref, p):
        i, a, z = PIECES[p]
        return ref.at[i, :, pl.ds(a, z - a)]

    def exch(i, step):
        return remote(exch_out.at[i], exch_in.at[i], ex_send.at[i], ex_recv.at[i], at(step))

    def send_g1(p):
        return remote(piece(g1_out, p), piece(g1_in, p), g1_send.at[p], g1_recv.at[p], at(-1))

    def send_g0(p):
        return remote(piece(g0_out, p), piece(g0_in, p), g0_send.at[p], g0_recv.at[p], at(-2))

    def y_copy(p, j):
        i, a, z = PIECES[p]
        to = pl.multiple_of(lax.rem(member + j, 4) * 32, 32)
        return remote(
            y_out.at[i, pl.ds(to, 32), pl.ds(a, z - a)], y_in.at[i, j - 1, :, pl.ds(a, z - a)],
            y_send.at[p, j - 1], y_recv.at[p, j - 1], peer(j),
        )

    def of(i):
        return [p for p in range(3) if PIECES[p][0] == i]

    def tails(b, i, parts):
        if b == 2:
            for a, z, x in parts:
                g0_out[i, :, a:z] = x.astype(bf16)

            @pl.when(even)
            def _():
                for p in of(i):
                    send_g0(p).start()

            @pl.when(odd)
            def _():
                exch_out[i] = g0_out[i]
                exch(i, -1).start()
        else:
            for a, z, x in parts:
                part[i, :, a:z] = x

            @pl.when(odd)
            def _():
                for p in of(i):
                    _, a, z = PIECES[p]
                    g1_out[i, :, a:z] = part[i, :, a:z].astype(bf16)
                    send_g1(p).start()

    def combine(i):
        exch(i, 1).wait_recv()
        for p in of(i):
            _, a, z = PIECES[p]
            g1_out[i, :, a:z] = (part[i, :, a:z] + exch_in[i, :, a:z].astype(f32)).astype(bf16)
            send_g1(p).start()

    score(0)
    dprob(0)

    @pl.when(has[-1])
    def _():
        hop1(0).wait_recv()

        @pl.when(even)
        def _():
            relay(0).start()
        score(1)

    @pl.when(has[-2])
    def _():
        recv2(0).wait_recv()
        score(2)

    coef(0)
    delta_s[0:1, :] = dl_s[0:1, :] * c_s[0, 0:1, :]

    @pl.when(has[-2])
    def _():
        coef(2)
        tails(2, 1, value_part(2))

    @pl.when(has[-1])
    def _():
        coef(1)
        tails(1, 1, value_part(1))
        hop1(1).wait_recv()

        @pl.when(even)
        def _():
            relay(1).start()
        dprob(1)

    @pl.when(has[-2])
    def _():
        recv2(1).wait_recv()
        dprob(2)

        @pl.when(even)
        def _():
            combine(1)
        tails(2, 0, key_part(2))

    @pl.when(has[-1])
    def _():
        tails(1, 0, key_part(1))

        @pl.when(even)
        def _():
            combine(0)

    for a, z, x in value_part(0):
        own[1, :, a:z] = x
    for a, z, x in key_part(0):
        own[0, :, a:z] = x

    def finish(p):
        i, a, z = PIECES[p]

        @pl.when(has[1])
        def _():
            send_g1(p).wait_recv()
            own[i, :, a:z] += g1_in[i, :, a:z].astype(f32)

        @pl.when(even & has[2])
        def _():
            send_g0(p).wait_recv()
            own[i, :, a:z] += g0_in[i, :, a:z].astype(f32)
        y_out[i, :, a:z] = own[i, :, a:z].astype(bf16)
        for j in (1, 2, 3):
            y_copy(p, j).start()

    finish(0)

    row_parts(0)

    @pl.when(has[-1])
    def _():
        row_parts(1)

    @pl.when(has[-2])
    def _():
        row_parts(2)

    for half in range(2):
        for h in range(2):
            c = half * T + h * H
            rows, lanes = slice(half * H, (half + 1) * H), slice(h * D, (h + 1) * D)
            o_vm[rows, lanes] = o_acc[:, c:c + H].T.astype(bf16)
            dq_vm[rows, lanes] = dq_s[:, c:c + H].T.astype(bf16)

    finish(1)
    finish(2)

    mine = pl.multiple_of(member * 32, 32)
    for p in range(3):
        i, a, z = PIECES[p]
        acc = own[i, pl.ds(mine, 32), a:z]
        for j in (1, 2, 3):
            y_copy(p, j).wait_recv()
            acc = acc + y_in[i, j - 1, :, a:z].astype(f32)
        (dk_ref, dv_ref)[i][:, a:z] = acc

    for i in (0, 1):
        @pl.when(has[1])
        def _(i=i):
            hop1(i).wait_send()

        @pl.when(even & has[2])
        def _(i=i):
            hop2(i).wait_send()

        @pl.when(even & has[-1])
        def _(i=i):
            relay(i).wait_send()

        @pl.when(odd & has[-2])
        def _(i=i):
            exch(i, -1).wait_send()

    for p in range(3):
        @pl.when(has[-1])
        def _(p=p):
            send_g1(p).wait_send()

        @pl.when(even & has[-2])
        def _(p=p):
            send_g0(p).wait_send()
        for j in (1, 2, 3):
            y_copy(p, j).wait_send()


def place(o, dq, dk, dv, o_out, dq_out, dk_out, dv_out, sem):
    pairs = ((o, o_out), (dq, dq_out), (dk, dk_out), (dv, dv_out))
    copies = [pltpu.make_async_copy(a, b, sem.at[i]) for i, (a, b) in enumerate(pairs)]
    for c in copies:
        c.start()
    for c in copies:
        c.wait()


def body(queries, keys, values, out_grad, doc_start):
    hbm = pl.BlockSpec(memory_space=pltpu.HBM)
    vmem = pl.BlockSpec(memory_space=pltpu.VMEM)
    V, DMA = pltpu.VMEM, pltpu.SemaphoreType.DMA
    S = jax.ShapeDtypeStruct
    o, dq, dk, dv = pl.pallas_call(
        kernel,
        out_shape=(S((T, 2 * D), bf16), S((T, 2 * D), bf16), S((32, T), f32), S((32, T), f32)),
        in_specs=[hbm] * 5,
        out_specs=(vmem,)*4,
        scratch_shapes=[
            V((T, 2 * D), bf16), V((T, 2 * D), bf16), V((1, T), jnp.int32), V((3, 2, T, D), bf16),
            V((2 * T, D), bf16), V((2 * T, D), bf16), V((D, 2 * T), bf16), V((D, 2 * T), bf16),
            V((3, T, 2 * T), bf16), V((3, T, 2 * T), f32), V((3, T, 2 * T), bf16),
            V((4, 8, 2 * T), f32), V((8, 2 * T), f32), V((8, 2 * T), f32), V((3, 8, 2 * T), f32),
            V((8, 2 * T), f32), V((D, 2 * T), f32), V((D, 2 * T), f32),
            V((2, D, T), f32), V((2, D, T), f32), V((2, D, T), bf16), V((2, D, T), bf16),
            V((2, D, T), bf16), V((2, D, T), bf16), V((2, D, T), bf16), V((2, D, T), bf16),
            V((2, D, T), bf16), V((2, 3, 32, T), bf16),
            DMA((5,)), DMA((2, 2)), DMA((3, 2)), DMA((2,)), DMA((2,)), DMA((2,)),
            DMA((3,)), DMA((3,)), DMA((3,)), DMA((3,)), DMA((3, 3)), DMA((3, 3)),
        ],
        compiler_params=pltpu.CompilerParams(
            collective_id=0, has_side_effects=True, vmem_limit_bytes=int(53.25 * 2**20)
        ),
    )(queries, keys, values, out_grad, pltpu.with_memory_space_constraint(doc_start.reshape(1, T), pltpu.HBM))
    o, dq, dk, dv = pl.pallas_call(
        place,
        out_shape=(S((T, 2 * D), bf16), S((T, 2 * D), bf16), S((32, T), f32), S((32, T), f32)),
        in_specs=[vmem] * 4,
        out_specs=(hbm,) * 4,
        scratch_shapes=[DMA((4,))],
        compiler_params=pltpu.CompilerParams(vmem_limit_bytes=4 * 2**20),
    )(o, dq, dk, dv)
    return o, dq, dk.T, dv.T


def solution(mesh):
    placed = (P("ctx", "head"), P("ctx", None), P("ctx", None), P("ctx", "head"), P("ctx"))
    return jax.shard_map(
        body,
        mesh=mesh,
        in_specs=placed,
        out_specs=(P("ctx", "head"),) * 4,
        check_vma=False,
    )
```

```python
import math

import jax
import jax.numpy as jnp
from jax import lax
from jax.experimental import pallas as pl
from jax.experimental.pallas import tpu as pltpu
from jax.sharding import PartitionSpec as P

D = 128
WINDOW = 1024
T = 512
H = 256
SCALE = D**-0.5
SCALE2 = SCALE * math.log2(math.e)
MESH = pl.DeviceIdType.MESH
f32, bf16 = jnp.float32, jnp.bfloat16

SEEN = {(0, 0): (0, H), (0, 1): (0, T), (1, 0): (0, T), (1, 1): (0, T), (2, 0): (0, T), (2, 1): (H, T)}


def dot(a, b, ca, cb):
    return lax.dot_general(a, b, (((ca,), (cb,)), ((), ())), preferred_element_type=f32)


PIECES = ((1, 0, T), (0, 0, H), (0, H, T))


def kernel(
    q_hbm, k_hbm, v_hbm, do_hbm, doc_hbm,
    o_vm, dq_vm, dk_ref, dv_ref,
    q_in, do_in, doc_ref, kv, q2, do2, q_t, do_t,
    e_s, dp_s, ds_s, m_s, l_s, dl_s, c_s, delta_s, o_acc, dq_s,
    own, part, exch_out, exch_in, g1_out, g0_out, g1_in, g0_in, y_out, y_in,
    in_sem, kv_send, kv_recv, relay_send, ex_send, ex_recv,
    g1_send, g1_recv, g0_send, g0_recv, y_send, y_recv, here,
):
    ctx = lax.axis_index("ctx")
    head = lax.axis_index("head")
    n_ctx = lax.axis_size("ctx")
    core = lax.rem(ctx, 2)
    even = core == 0
    odd = core == 1
    group = head // 4
    member = lax.rem(head, 4)

    def at(step):
        return (ctx + step, head)

    def peer(j):
        return (ctx, group * 4 + lax.rem(member + j, 4))

    def remote(src, dst, ss, rs, dev):
        return pltpu.make_async_remote_copy(
            src_ref=src, dst_ref=dst, send_sem=ss, recv_sem=rs,
            device_id=dev, device_id_type=MESH,
        )

    source = (k_hbm, v_hbm)
    cols = pl.ds(pl.multiple_of(group * D, D), D)
    loads = [
        pltpu.make_async_copy(k_hbm.at[:, cols], kv.at[0, 0], in_sem.at[0]),
        pltpu.make_async_copy(v_hbm.at[:, cols], kv.at[0, 1], in_sem.at[1]),
        pltpu.make_async_copy(q_hbm, q_in, in_sem.at[2]),
        pltpu.make_async_copy(do_hbm, do_in, in_sem.at[3]),
        pltpu.make_async_copy(doc_hbm, doc_ref, in_sem.at[4]),
    ]
    for c in loads:
        c.start()

    has = {-2: ctx >= 2, -1: ctx >= 1, 1: ctx < n_ctx - 1, 2: ctx < n_ctx - 2}
    barrier = pltpu.get_barrier_semaphore()
    up, down = member < 3, member > 0

    def beside(step):
        return (ctx, head + step)

    def signal(sem, dev):
        pl.semaphore_signal(sem, inc=1, device_id=dev, device_id_type=MESH)

    @pl.when(has[-1])
    def _():
        signal(barrier, at(-1))

    @pl.when(even & has[-2])
    def _():
        signal(barrier, at(-2))

    @pl.when(up)
    def _():
        signal(barrier, beside(1))

    @pl.when(down)
    def _():
        signal(barrier, beside(-1))

    greeters = (has[1], even & has[2], up, down)
    pl.semaphore_wait(barrier, sum(g.astype(jnp.int32) for g in greeters))

    def hop1(i):
        return remote(source[i].at[:, cols], kv.at[1, i], kv_send.at[0, i], kv_recv.at[1, i], at(1))

    def hop2(i):
        return remote(source[i].at[:, cols], kv.at[2, i], kv_send.at[1, i], kv_recv.at[2, i], at(2))

    def relay(i):
        return remote(kv.at[1, i], kv.at[2, i], relay_send.at[i], kv_recv.at[2, i], at(1))

    def recv2(i):
        return remote(kv.at[0, i], kv.at[2, i], kv_send.at[1, i], kv_recv.at[2, i], at(2))

    for i in (0, 1):
        @pl.when(has[1])
        def _(i=i):
            hop1(i).start()

        @pl.when(even & has[2])
        def _(i=i):
            hop2(i).start()

    @pl.when(up & down)
    def _():
        signal(here.at[0], beside(-1))
        signal(here.at[1], beside(1))

    loads[2].wait()
    loads[3].wait()
    loads[4].wait()
    loads[0].wait()
    loads[1].wait()
    for half in range(2):
        for h in range(2):
            c = half * T + h * H
            a = q_in[half * H:(half + 1) * H, h * D:(h + 1) * D]
            q2[c:c + H, :] = a
            q_t[:, c:c + H] = a.T
            a = do_in[half * H:(half + 1) * H, h * D:(h + 1) * D]
            do2[c:c + H, :] = a
            do_t[:, c:c + H] = a.T

    doc = doc_ref[0:1, :] - ctx * T

    def score(b):
        for half in range(2):
            lo_k, hi_k = SEEN[b, half]
            n = hi_k - lo_k
            c0 = half * T
            s = dot(kv[b, 0, lo_k:hi_k, :], q2[c0:c0 + T, :], 1, 1) * SCALE2
            key_pos = lax.broadcasted_iota(jnp.int32, (n, H), 0) + (lo_k - b * T)
            query_pos = lax.broadcasted_iota(jnp.int32, (1, H), 1) + half * H
            first = jnp.maximum(query_pos - (WINDOW - 1), doc[:, half * H:(half + 1) * H])
            visible = key_pos >= first
            if b == 0:
                visible = visible & (key_pos <= query_pos)
            visible = jnp.concatenate([visible, visible], axis=1)
            s = jnp.where(visible, s, -1e30)
            m = jnp.max(s, axis=0, keepdims=True)
            if b > 0:
                m_old = m_s[3, 0:1, c0:c0 + T]
                m = jnp.maximum(m_old, m)
            e = jnp.exp2(s - m)
            l = jnp.sum(e, axis=0, keepdims=True)
            if b > 0:
                l = l + jnp.exp2(m_old - m) * l_s[0:1, c0:c0 + T]
            m_s[b, 0:1, c0:c0 + T] = m
            m_s[3, 0:1, c0:c0 + T] = m
            l_s[0:1, c0:c0 + T] = l
            e_s[b, lo_k:hi_k, c0:c0 + T] = e.astype(bf16)

    def dprob(b):
        for half in range(2):
            lo_k, hi_k = SEEN[b, half]
            c0 = half * T
            dp = dot(kv[b, 1, lo_k:hi_k, :], do2[c0:c0 + T, :], 1, 1)
            dp_s[b, lo_k:hi_k, c0:c0 + T] = dp
            e = e_s[b, lo_k:hi_k, c0:c0 + T].astype(f32)
            dl = jnp.sum(e * dp, axis=0, keepdims=True)
            if b < 2:
                dl_s[b, 0:1, c0:c0 + T] = dl
            else:
                delta_s[0:1, c0:c0 + T] += dl * c_s[b, 0:1, c0:c0 + T]

    def coef(b):
        c_s[b, 0:1, :] = jnp.exp2(m_s[b, 0:1, :] - m_s[3, 0:1, :]) / l_s[0:1, :]

    def assemble(b, p):
        if b == 0:
            return [(0, H, p[0] + p[1][:, :H]), (H, T, p[1][:, H:])]
        if b == 1:
            return [(0, T, p[0] + p[1])]
        return [(0, H, p[0][:, :H]), (H, T, p[0][:, H:] + p[1])]

    def value_part(b):
        w = (do_t[...].astype(f32) * c_s[b, 0:1, :]).astype(bf16)
        parts = []
        for half in range(2):
            lo_k, hi_k = SEEN[b, half]
            c0 = half * T
            parts.append(dot(w[:, c0:c0 + T], e_s[b, lo_k:hi_k, c0:c0 + T], 1, 1))
        return assemble(b, parts)

    def key_part(b):
        w = (q_t[...].astype(f32) * (c_s[b, 0:1, :] * SCALE)).astype(bf16)
        parts = []
        for half in range(2):
            lo_k, hi_k = SEEN[b, half]
            c0 = half * T
            ds = e_s[b, lo_k:hi_k, c0:c0 + T].astype(f32)
            ds = (ds * (dp_s[b, lo_k:hi_k, c0:c0 + T] - delta_s[0:1, c0:c0 + T])).astype(bf16)
            ds_s[b, lo_k:hi_k, c0:c0 + T] = ds
            parts.append(dot(w[:, c0:c0 + T], ds, 1, 1))
        return assemble(b, parts)

    def row_parts(b):
        k_t, v_t = kv[b, 0].T, kv[b, 1].T
        for half in range(2):
            lo_k, hi_k = SEEN[b, half]
            c0 = half * T
            c = c_s[b, 0:1, c0:c0 + T]
            o = dot(v_t[:, lo_k:hi_k], e_s[b, lo_k:hi_k, c0:c0 + T], 1, 0) * c
            dq = dot(k_t[:, lo_k:hi_k], ds_s[b, lo_k:hi_k, c0:c0 + T], 1, 0) * (c * SCALE)
            if b == 0:
                o_acc[:, c0:c0 + T] = o
                dq_s[:, c0:c0 + T] = dq
            else:
                o_acc[:, c0:c0 + T] += o
                dq_s[:, c0:c0 + T] += dq

    def piece(ref, p):
        i, a, z = PIECES[p]
        return ref.at[i, :, pl.ds(a, z - a)]

    def exch(i, step):
        return remote(exch_out.at[i], exch_in.at[i], ex_send.at[i], ex_recv.at[i], at(step))

    def send_g1(p):
        return remote(piece(g1_out, p), piece(g1_in, p), g1_send.at[p], g1_recv.at[p], at(-1))

    def send_g0(p):
        return remote(piece(g0_out, p), piece(g0_in, p), g0_send.at[p], g0_recv.at[p], at(-2))

    def y_copy(p, j):
        i, a, z = PIECES[p]
        to = pl.multiple_of(lax.rem(member + j, 4) * 32, 32)
        return remote(
            y_out.at[i, pl.ds(to, 32), pl.ds(a, z - a)], y_in.at[i, j - 1, :, pl.ds(a, z - a)],
            y_send.at[p, j - 1], y_recv.at[p, j - 1], peer(j),
        )

    def of(i):
        return [p for p in range(3) if PIECES[p][0] == i]

    def tails(b, i, parts):
        if b == 2:
            for a, z, x in parts:
                g0_out[i, :, a:z] = x.astype(bf16)

            @pl.when(even)
            def _():
                for p in of(i):
                    send_g0(p).start()

            @pl.when(odd)
            def _():
                exch_out[i] = g0_out[i]
                exch(i, -1).start()
        else:
            for a, z, x in parts:
                part[i, :, a:z] = x

            @pl.when(odd)
            def _():
                for p in of(i):
                    _, a, z = PIECES[p]
                    g1_out[i, :, a:z] = part[i, :, a:z].astype(bf16)
                    send_g1(p).start()

    def combine(i):
        exch(i, 1).wait_recv()
        for p in of(i):
            _, a, z = PIECES[p]
            g1_out[i, :, a:z] = (part[i, :, a:z] + exch_in[i, :, a:z].astype(f32)).astype(bf16)
            send_g1(p).start()

    score(0)
    dprob(0)

    @pl.when(has[-1])
    def _():
        for i in (0, 1):
            hop1(i).wait_recv()

            @pl.when(even)
            def _(i=i):
                relay(i).start()
            (score, dprob)[i](1)

    @pl.when(has[-2])
    def _():
        recv2(0).wait_recv()
        score(2)
        coef(2)
        tails(2, 1, value_part(2))

    coef(0)
    delta_s[0:1, :] = dl_s[0, 0:1, :] * c_s[0, 0:1, :]

    @pl.when(has[-1])
    def _():
        coef(1)
        tails(1, 1, value_part(1))
        delta_s[0:1, :] += dl_s[1, 0:1, :] * c_s[1, 0:1, :]

    @pl.when(has[-2])
    def _():
        @pl.when(even)
        def _():
            combine(1)
        recv2(1).wait_recv()
        dprob(2)
        tails(2, 0, key_part(2))

    @pl.when(has[-1])
    def _():
        tails(1, 0, key_part(1))

        @pl.when(even & has[-2])
        def _():
            combine(0)

    for a, z, x in value_part(0):
        own[1, :, a:z] = x
    for a, z, x in key_part(0):
        own[0, :, a:z] = x

    def finish(p):
        i, a, z = PIECES[p]

        @pl.when(has[1])
        def _():
            send_g1(p).wait_recv()
            own[i, :, a:z] += g1_in[i, :, a:z].astype(f32)

        @pl.when(even & has[2])
        def _():
            send_g0(p).wait_recv()
            own[i, :, a:z] += g0_in[i, :, a:z].astype(f32)
        y_out[i, :, a:z] = own[i, :, a:z].astype(bf16)

        @pl.when(member < 2)
        def _():
            for j in (3, 2, 1):
                y_copy(p, j).start()

        @pl.when(member >= 2)
        def _():
            for j in (1, 2, 3):
                y_copy(p, j).start()

    @pl.when(member == 1)
    def _():
        pl.semaphore_wait(here.at[0], 1)
        signal(here.at[2], beside(-1))

    @pl.when(member == 2)
    def _():
        pl.semaphore_wait(here.at[1], 1)
        signal(here.at[2], beside(1))

    row_parts(0)

    @pl.when(has[-1])
    def _():
        row_parts(1)

    @pl.when(has[-2])
    def _():
        row_parts(2)

    for half in range(2):
        for h in range(2):
            c = half * T + h * H
            rows, lanes = slice(half * H, (half + 1) * H), slice(h * D, (h + 1) * D)
            o_vm[rows, lanes] = o_acc[:, c:c + H].T.astype(bf16)
            dq_vm[rows, lanes] = dq_s[:, c:c + H].T.astype(bf16)

    @pl.when(member == 0)
    def _():
        pl.semaphore_wait(here.at[0], 1)
        pl.semaphore_wait(here.at[2], 1)

    @pl.when(member == 3)
    def _():
        pl.semaphore_wait(here.at[1], 1)
        pl.semaphore_wait(here.at[2], 1)

    for p in range(3):
        finish(p)

    mine = pl.multiple_of(member * 32, 32)
    for p in range(3):
        i, a, z = PIECES[p]
        acc = own[i, pl.ds(mine, 32), a:z]
        for j in (1, 2, 3):
            y_copy(p, j).wait_recv()
            acc = acc + y_in[i, j - 1, :, a:z].astype(f32)
        (dk_ref, dv_ref)[i][:, a:z] = acc

    for i in (0, 1):
        @pl.when(has[1])
        def _(i=i):
            hop1(i).wait_send()

        @pl.when(even & has[2])
        def _(i=i):
            hop2(i).wait_send()

        @pl.when(even & has[-1])
        def _(i=i):
            relay(i).wait_send()

        @pl.when(odd & has[-2])
        def _(i=i):
            exch(i, -1).wait_send()

    for p in range(3):
        @pl.when(has[-1])
        def _(p=p):
            send_g1(p).wait_send()

        @pl.when(even & has[-2])
        def _(p=p):
            send_g0(p).wait_send()
        for j in (1, 2, 3):
            y_copy(p, j).wait_send()


def place(o, dq, dk, dv, o_out, dq_out, dk_out, dv_out, sem):
    pairs = ((o, o_out), (dq, dq_out), (dk, dk_out), (dv, dv_out))
    copies = [pltpu.make_async_copy(a, b, sem.at[i]) for i, (a, b) in enumerate(pairs)]
    for c in copies:
        c.start()
    for c in copies:
        c.wait()


def body(queries, keys, values, out_grad, doc_start):
    hbm = pl.BlockSpec(memory_space=pltpu.HBM)
    vmem = pl.BlockSpec(memory_space=pltpu.VMEM)
    V, DMA = pltpu.VMEM, pltpu.SemaphoreType.DMA
    S = jax.ShapeDtypeStruct
    o, dq, dk, dv = pl.pallas_call(
        kernel,
        out_shape=(S((T, 2 * D), bf16), S((T, 2 * D), bf16), S((32, T), f32), S((32, T), f32)),
        in_specs=[hbm] * 5,
        out_specs=(vmem,)*4,
        scratch_shapes=[
            V((T, 2 * D), bf16), V((T, 2 * D), bf16), V((1, T), jnp.int32), V((3, 2, T, D), bf16),
            V((2 * T, D), bf16), V((2 * T, D), bf16), V((D, 2 * T), bf16), V((D, 2 * T), bf16),
            V((3, T, 2 * T), bf16), V((3, T, 2 * T), f32), V((3, T, 2 * T), bf16),
            V((4, 8, 2 * T), f32), V((8, 2 * T), f32), V((2, 8, 2 * T), f32), V((3, 8, 2 * T), f32),
            V((8, 2 * T), f32), V((D, 2 * T), f32), V((D, 2 * T), f32),
            V((2, D, T), f32), V((2, D, T), f32), V((2, D, T), bf16), V((2, D, T), bf16),
            V((2, D, T), bf16), V((2, D, T), bf16), V((2, D, T), bf16), V((2, D, T), bf16),
            V((2, D, T), bf16), V((2, 3, 32, T), bf16),
            DMA((5,)), DMA((2, 2)), DMA((3, 2)), DMA((2,)), DMA((2,)), DMA((2,)),
            DMA((3,)), DMA((3,)), DMA((3,)), DMA((3,)), DMA((3, 3)), DMA((3, 3)),
            pltpu.SemaphoreType.REGULAR((3,)),
        ],
        compiler_params=pltpu.CompilerParams(
            collective_id=0, has_side_effects=True, vmem_limit_bytes=int(53.25 * 2**20)
        ),
    )(queries, keys, values, out_grad, pltpu.with_memory_space_constraint(doc_start.reshape(1, T), pltpu.HBM))
    o, dq, dk, dv = pl.pallas_call(
        place,
        out_shape=(S((T, 2 * D), bf16), S((T, 2 * D), bf16), S((32, T), f32), S((32, T), f32)),
        in_specs=[vmem] * 4,
        out_specs=(hbm,) * 4,
        scratch_shapes=[DMA((4,))],
        compiler_params=pltpu.CompilerParams(vmem_limit_bytes=4 * 2**20),
    )(o, dq, dk, dv)
    return o, dq, dk.T, dv.T


def solution(mesh):
    placed = (P("ctx", "head"), P("ctx", None), P("ctx", None), P("ctx", "head"), P("ctx"))
    return jax.shard_map(
        body,
        mesh=mesh,
        in_specs=placed,
        out_specs=(P("ctx", "head"),) * 4,
        check_vma=False,
    )
```

```python
import math

import jax
import jax.numpy as jnp
from jax import lax
from jax.experimental import pallas as pl
from jax.experimental.pallas import tpu as pltpu
from jax.sharding import PartitionSpec as P

D = 128
WINDOW = 1024
T = 512
H = 256
SCALE = D**-0.5
SCALE2 = SCALE * math.log2(math.e)
MESH = pl.DeviceIdType.MESH
f32, bf16 = jnp.float32, jnp.bfloat16

SEEN = {(0, 0): (0, H), (0, 1): (0, T), (1, 0): (0, T), (1, 1): (0, T), (2, 0): (0, T), (2, 1): (H, T)}


def dot(a, b, ca, cb):
    return lax.dot_general(a, b, (((ca,), (cb,)), ((), ())), preferred_element_type=f32)


PIECES = ((1, 0, T), (0, 0, H), (0, H, T))


def kernel(
    q_hbm, k_hbm, v_hbm, do_hbm, doc_hbm,
    o_vm, dq_vm, dk_ref, dv_ref,
    q_in, do_in, doc_ref, kv, q2, do2, q_t, do_t,
    e_s, dp_s, ds_s, m_s, l_s, c_s, delta_s, o_acc, dq_s,
    own, part, exch_out, exch_in, g1_out, g0_out, g1_in, g0_in, y_out, y_in,
    in_sem, kv_send, kv_recv, relay_send, ex_send, ex_recv,
    g1_send, g1_recv, g0_send, g0_recv, y_send, y_recv, here,
):
    ctx = lax.axis_index("ctx")
    head = lax.axis_index("head")
    n_ctx = lax.axis_size("ctx")
    core = lax.rem(ctx, 2)
    even = core == 0
    odd = core == 1
    group = head // 4
    member = lax.rem(head, 4)

    def at(step):
        return (ctx + step, head)

    def peer(j):
        return (ctx, group * 4 + lax.rem(member + j, 4))

    def remote(src, dst, ss, rs, dev):
        return pltpu.make_async_remote_copy(
            src_ref=src, dst_ref=dst, send_sem=ss, recv_sem=rs,
            device_id=dev, device_id_type=MESH,
        )

    source = (k_hbm, v_hbm)
    cols = pl.ds(pl.multiple_of(group * D, D), D)
    loads = [
        pltpu.make_async_copy(k_hbm.at[:, cols], kv.at[0, 0], in_sem.at[0]),
        pltpu.make_async_copy(v_hbm.at[:, cols], kv.at[0, 1], in_sem.at[1]),
        pltpu.make_async_copy(q_hbm, q_in, in_sem.at[2]),
        pltpu.make_async_copy(do_hbm, do_in, in_sem.at[3]),
        pltpu.make_async_copy(doc_hbm, doc_ref, in_sem.at[4]),
    ]
    for c in loads:
        c.start()

    has = {-2: ctx >= 2, -1: ctx >= 1, 1: ctx < n_ctx - 1, 2: ctx < n_ctx - 2}
    barrier = pltpu.get_barrier_semaphore()
    up, down = member < 3, member > 0

    def beside(step):
        return (ctx, head + step)

    def signal(sem, dev):
        pl.semaphore_signal(sem, inc=1, device_id=dev, device_id_type=MESH)

    @pl.when(has[-1])
    def _():
        signal(barrier, at(-1))

    @pl.when(even & has[-2])
    def _():
        signal(barrier, at(-2))

    @pl.when(up)
    def _():
        signal(barrier, beside(1))

    @pl.when(down)
    def _():
        signal(barrier, beside(-1))

    greeters = (has[1], even & has[2], up, down)
    pl.semaphore_wait(barrier, sum(g.astype(jnp.int32) for g in greeters))

    def hop1(i):
        return remote(source[i].at[:, cols], kv.at[1, i], kv_send.at[0, i], kv_recv.at[1, i], at(1))

    def hop2(i):
        return remote(source[i].at[:, cols], kv.at[2, i], kv_send.at[1, i], kv_recv.at[2, i], at(2))

    def relay(i):
        return remote(kv.at[1, i], kv.at[2, i], relay_send.at[i], kv_recv.at[2, i], at(1))

    def recv2(i):
        return remote(kv.at[0, i], kv.at[2, i], kv_send.at[1, i], kv_recv.at[2, i], at(2))

    for i in (0, 1):
        @pl.when(has[1])
        def _(i=i):
            hop1(i).start()

        @pl.when(even & has[2])
        def _(i=i):
            hop2(i).start()

    @pl.when(up & down)
    def _():
        signal(here.at[0], beside(-1))
        signal(here.at[1], beside(1))

    loads[2].wait()
    loads[3].wait()
    loads[4].wait()
    loads[0].wait()
    loads[1].wait()
    for half in range(2):
        for h in range(2):
            c = half * T + h * H
            a = q_in[half * H:(half + 1) * H, h * D:(h + 1) * D]
            q2[c:c + H, :] = a
            q_t[:, c:c + H] = a.T
            a = do_in[half * H:(half + 1) * H, h * D:(h + 1) * D]
            do2[c:c + H, :] = a
            do_t[:, c:c + H] = a.T

    doc = doc_ref[0:1, :] - ctx * T

    def score(b):
        for half in range(2):
            lo_k, hi_k = SEEN[b, half]
            n = hi_k - lo_k
            c0 = half * T
            s = dot(kv[b, 0, lo_k:hi_k, :], q2[c0:c0 + T, :], 1, 1) * SCALE2
            key_pos = lax.broadcasted_iota(jnp.int32, (n, H), 0) + (lo_k - b * T)
            query_pos = lax.broadcasted_iota(jnp.int32, (1, H), 1) + half * H
            first = jnp.maximum(query_pos - (WINDOW - 1), doc[:, half * H:(half + 1) * H])
            visible = key_pos >= first
            if b == 0:
                visible = visible & (key_pos <= query_pos)
            visible = jnp.concatenate([visible, visible], axis=1)
            s = jnp.where(visible, s, -1e30)
            m = jnp.max(s, axis=0, keepdims=True)
            if b > 0:
                m_old = m_s[3, 0:1, c0:c0 + T]
                m = jnp.maximum(m_old, m)
            e = jnp.exp2(s - m)
            l = jnp.sum(e, axis=0, keepdims=True)
            if b > 0:
                l = l + jnp.exp2(m_old - m) * l_s[0:1, c0:c0 + T]
            m_s[b, 0:1, c0:c0 + T] = m
            m_s[3, 0:1, c0:c0 + T] = m
            l_s[0:1, c0:c0 + T] = l
            e_s[b, lo_k:hi_k, c0:c0 + T] = e.astype(bf16)

    def dprob(b):
        for half in range(2):
            lo_k, hi_k = SEEN[b, half]
            c0 = half * T
            dp = dot(kv[b, 1, lo_k:hi_k, :], do2[c0:c0 + T, :], 1, 1)
            dp_s[b, lo_k:hi_k, c0:c0 + T] = dp
            e = e_s[b, lo_k:hi_k, c0:c0 + T].astype(f32)
            dl = jnp.sum(e * dp, axis=0, keepdims=True)
            dl = dl * c_s[b, 0:1, c0:c0 + T]
            if b == 0:
                delta_s[0:1, c0:c0 + T] = dl
            else:
                delta_s[0:1, c0:c0 + T] += dl

    def coef(b):
        c_s[b, 0:1, :] = jnp.exp2(m_s[b, 0:1, :] - m_s[3, 0:1, :]) / l_s[0:1, :]

    def assemble(b, p):
        if b == 0:
            return [(0, H, p[0] + p[1][:, :H]), (H, T, p[1][:, H:])]
        if b == 1:
            return [(0, T, p[0] + p[1])]
        return [(0, H, p[0][:, :H]), (H, T, p[0][:, H:] + p[1])]

    def value_part(b):
        w = (do_t[...].astype(f32) * c_s[b, 0:1, :]).astype(bf16)
        parts = []
        for half in range(2):
            lo_k, hi_k = SEEN[b, half]
            c0 = half * T
            parts.append(dot(w[:, c0:c0 + T], e_s[b, lo_k:hi_k, c0:c0 + T], 1, 1))
        return assemble(b, parts)

    def key_part(b):
        w = (q_t[...].astype(f32) * (c_s[b, 0:1, :] * SCALE)).astype(bf16)
        parts = []
        for half in range(2):
            lo_k, hi_k = SEEN[b, half]
            c0 = half * T
            ds = e_s[b, lo_k:hi_k, c0:c0 + T].astype(f32)
            ds = (ds * (dp_s[b, lo_k:hi_k, c0:c0 + T] - delta_s[0:1, c0:c0 + T])).astype(bf16)
            ds_s[b, lo_k:hi_k, c0:c0 + T] = ds
            parts.append(dot(w[:, c0:c0 + T], ds, 1, 1))
        return assemble(b, parts)

    def row_parts(b):
        k_t, v_t = kv[b, 0].T, kv[b, 1].T
        for half in range(2):
            lo_k, hi_k = SEEN[b, half]
            c0 = half * T
            c = c_s[b, 0:1, c0:c0 + T]
            o = dot(v_t[:, lo_k:hi_k], e_s[b, lo_k:hi_k, c0:c0 + T], 1, 0) * c
            dq = dot(k_t[:, lo_k:hi_k], ds_s[b, lo_k:hi_k, c0:c0 + T], 1, 0) * (c * SCALE)
            if b == 0:
                o_acc[:, c0:c0 + T] = o
                dq_s[:, c0:c0 + T] = dq
            else:
                o_acc[:, c0:c0 + T] += o
                dq_s[:, c0:c0 + T] += dq

    def piece(ref, p):
        i, a, z = PIECES[p]
        return ref.at[i, :, pl.ds(a, z - a)]

    def exch(i, step):
        return remote(exch_out.at[i], exch_in.at[i], ex_send.at[i], ex_recv.at[i], at(step))

    def send_g1(p):
        return remote(piece(g1_out, p), piece(g1_in, p), g1_send.at[p], g1_recv.at[p], at(-1))

    def send_g0(p):
        return remote(piece(g0_out, p), piece(g0_in, p), g0_send.at[p], g0_recv.at[p], at(-2))

    def y_copy(p, j):
        i, a, z = PIECES[p]
        to = pl.multiple_of(lax.rem(member + j, 4) * 32, 32)
        return remote(
            y_out.at[i, pl.ds(to, 32), pl.ds(a, z - a)], y_in.at[i, j - 1, :, pl.ds(a, z - a)],
            y_send.at[p, j - 1], y_recv.at[p, j - 1], peer(j),
        )

    def of(i):
        return [p for p in range(3) if PIECES[p][0] == i]

    def tails(b, i, parts):
        if b == 2:
            for a, z, x in parts:
                g0_out[i, :, a:z] = x.astype(bf16)

            @pl.when(even)
            def _():
                for p in of(i):
                    send_g0(p).start()

            @pl.when(odd)
            def _():
                exch_out[i] = g0_out[i]
                exch(i, -1).start()
        else:
            for a, z, x in parts:
                part[i, :, a:z] = x

            @pl.when(odd)
            def _():
                for p in of(i):
                    _, a, z = PIECES[p]
                    g1_out[i, :, a:z] = part[i, :, a:z].astype(bf16)
                    send_g1(p).start()

    def combine(i):
        exch(i, 1).wait_recv()
        for p in of(i):
            _, a, z = PIECES[p]
            g1_out[i, :, a:z] = (part[i, :, a:z] + exch_in[i, :, a:z].astype(f32)).astype(bf16)
            send_g1(p).start()

    score(0)

    @pl.when(has[-1])
    def _():
        hop1(0).wait_recv()

        @pl.when(even)
        def _():
            relay(0).start()
        score(1)

    @pl.when(has[-2])
    def _():
        recv2(0).wait_recv()
        score(2)
        coef(2)
        tails(2, 1, value_part(2))

    @pl.when(has[-1])
    def _():
        coef(1)
        tails(1, 1, value_part(1))

    coef(0)
    dprob(0)

    @pl.when(has[-1])
    def _():
        hop1(1).wait_recv()

        @pl.when(even)
        def _():
            relay(1).start()
        dprob(1)

    @pl.when(has[-2])
    def _():
        @pl.when(even)
        def _():
            combine(1)
        recv2(1).wait_recv()
        dprob(2)
        tails(2, 0, key_part(2))

    @pl.when(has[-1])
    def _():
        tails(1, 0, key_part(1))

        @pl.when(even & has[-2])
        def _():
            combine(0)

    for a, z, x in value_part(0):
        own[1, :, a:z] = x
    for a, z, x in key_part(0):
        own[0, :, a:z] = x

    def finish(p):
        i, a, z = PIECES[p]

        @pl.when(has[1])
        def _():
            send_g1(p).wait_recv()
            own[i, :, a:z] += g1_in[i, :, a:z].astype(f32)

        @pl.when(even & has[2])
        def _():
            send_g0(p).wait_recv()
            own[i, :, a:z] += g0_in[i, :, a:z].astype(f32)
        y_out[i, :, a:z] = own[i, :, a:z].astype(bf16)

        @pl.when(member < 2)
        def _():
            for j in (3, 2, 1):
                y_copy(p, j).start()

        @pl.when(member >= 2)
        def _():
            for j in (1, 2, 3):
                y_copy(p, j).start()

    @pl.when(member == 1)
    def _():
        pl.semaphore_wait(here.at[0], 1)
        signal(here.at[2], beside(-1))

    @pl.when(member == 2)
    def _():
        pl.semaphore_wait(here.at[1], 1)
        signal(here.at[2], beside(1))

    row_parts(0)

    @pl.when(has[-1])
    def _():
        row_parts(1)

    @pl.when(has[-2])
    def _():
        row_parts(2)

    for half in range(2):
        for h in range(2):
            c = half * T + h * H
            rows, lanes = slice(half * H, (half + 1) * H), slice(h * D, (h + 1) * D)
            o_vm[rows, lanes] = o_acc[:, c:c + H].T.astype(bf16)
            dq_vm[rows, lanes] = dq_s[:, c:c + H].T.astype(bf16)

    @pl.when(member == 0)
    def _():
        pl.semaphore_wait(here.at[0], 1)
        pl.semaphore_wait(here.at[2], 1)

    @pl.when(member == 3)
    def _():
        pl.semaphore_wait(here.at[1], 1)
        pl.semaphore_wait(here.at[2], 1)

    for p in range(3):
        finish(p)

    mine = pl.multiple_of(member * 32, 32)
    for p in range(3):
        i, a, z = PIECES[p]
        acc = own[i, pl.ds(mine, 32), a:z]
        for j in (1, 2, 3):
            y_copy(p, j).wait_recv()
            acc = acc + y_in[i, j - 1, :, a:z].astype(f32)
        (dk_ref, dv_ref)[i][:, a:z] = acc

    for i in (0, 1):
        @pl.when(has[1])
        def _(i=i):
            hop1(i).wait_send()

        @pl.when(even & has[2])
        def _(i=i):
            hop2(i).wait_send()

        @pl.when(even & has[-1])
        def _(i=i):
            relay(i).wait_send()

        @pl.when(odd & has[-2])
        def _(i=i):
            exch(i, -1).wait_send()

    for p in range(3):
        @pl.when(has[-1])
        def _(p=p):
            send_g1(p).wait_send()

        @pl.when(even & has[-2])
        def _(p=p):
            send_g0(p).wait_send()
        for j in (1, 2, 3):
            y_copy(p, j).wait_send()


def place(o, dq, dk, dv, o_out, dq_out, dk_out, dv_out, sem):
    pairs = ((o, o_out), (dq, dq_out), (dk, dk_out), (dv, dv_out))
    copies = [pltpu.make_async_copy(a, b, sem.at[i]) for i, (a, b) in enumerate(pairs)]
    for c in copies:
        c.start()
    for c in copies:
        c.wait()


def body(queries, keys, values, out_grad, doc_start):
    hbm = pl.BlockSpec(memory_space=pltpu.HBM)
    vmem = pl.BlockSpec(memory_space=pltpu.VMEM)
    V, DMA = pltpu.VMEM, pltpu.SemaphoreType.DMA
    S = jax.ShapeDtypeStruct
    o, dq, dk, dv = pl.pallas_call(
        kernel,
        out_shape=(S((T, 2 * D), bf16), S((T, 2 * D), bf16), S((32, T), f32), S((32, T), f32)),
        in_specs=[hbm] * 5,
        out_specs=(vmem,)*4,
        scratch_shapes=[
            V((T, 2 * D), bf16), V((T, 2 * D), bf16), V((1, T), jnp.int32), V((3, 2, T, D), bf16),
            V((2 * T, D), bf16), V((2 * T, D), bf16), V((D, 2 * T), bf16), V((D, 2 * T), bf16),
            V((3, T, 2 * T), bf16), V((3, T, 2 * T), f32), V((3, T, 2 * T), bf16),
            V((4, 8, 2 * T), f32), V((8, 2 * T), f32), V((3, 8, 2 * T), f32),
            V((8, 2 * T), f32), V((D, 2 * T), f32), V((D, 2 * T), f32),
            V((2, D, T), f32), V((2, D, T), f32), V((2, D, T), bf16), V((2, D, T), bf16),
            V((2, D, T), bf16), V((2, D, T), bf16), V((2, D, T), bf16), V((2, D, T), bf16),
            V((2, D, T), bf16), V((2, 3, 32, T), bf16),
            DMA((5,)), DMA((2, 2)), DMA((3, 2)), DMA((2,)), DMA((2,)), DMA((2,)),
            DMA((3,)), DMA((3,)), DMA((3,)), DMA((3,)), DMA((3, 3)), DMA((3, 3)),
            pltpu.SemaphoreType.REGULAR((3,)),
        ],
        compiler_params=pltpu.CompilerParams(
            collective_id=0, has_side_effects=True, vmem_limit_bytes=int(53.25 * 2**20)
        ),
    )(queries, keys, values, out_grad, pltpu.with_memory_space_constraint(doc_start.reshape(1, T), pltpu.HBM))
    o, dq, dk, dv = pl.pallas_call(
        place,
        out_shape=(S((T, 2 * D), bf16), S((T, 2 * D), bf16), S((32, T), f32), S((32, T), f32)),
        in_specs=[vmem] * 4,
        out_specs=(hbm,) * 4,
        scratch_shapes=[DMA((4,))],
        compiler_params=pltpu.CompilerParams(vmem_limit_bytes=4 * 2**20),
    )(o, dq, dk, dv)
    return o, dq, dk.T, dv.T


def solution(mesh):
    placed = (P("ctx", "head"), P("ctx", None), P("ctx", None), P("ctx", "head"), P("ctx"))
    return jax.shard_map(
        body,
        mesh=mesh,
        in_specs=placed,
        out_specs=(P("ctx", "head"),) * 4,
        check_vma=False,
    )
```

```python
import math

import jax
import jax.numpy as jnp
from jax import lax
from jax.experimental import pallas as pl
from jax.experimental.pallas import tpu as pltpu
from jax.sharding import PartitionSpec as P

D = 128
WINDOW = 1024
T = 512
H = 256
SCALE = D**-0.5
SCALE2 = SCALE * math.log2(math.e)
MESH = pl.DeviceIdType.MESH
f32, bf16 = jnp.float32, jnp.bfloat16

SEEN = {(0, 0): (0, H), (0, 1): (0, T), (1, 0): (0, T), (1, 1): (0, T), (2, 0): (0, T), (2, 1): (H, T)}


def dot(a, b, ca, cb):
    return lax.dot_general(a, b, (((ca,), (cb,)), ((), ())), preferred_element_type=f32)


PIECES = ((1, 0, T), (0, 0, H), (0, H, T))


def kernel(
    q_hbm, k_hbm, v_hbm, do_hbm, doc_hbm,
    o_vm, dq_vm, dk_ref, dv_ref,
    q_in, do_in, doc_ref, kv, q2, do2, q_t, do_t,
    e_s, dp_s, ds_s, m_s, l_s, c_s, delta_s, o_acc, dq_s,
    own, part, exch_out, exch_in, g1_out, g0_out, g1_in, g0_in, y_out, y_in,
    in_sem, kv_send, kv_recv, relay_send, ex_send, ex_recv,
    g1_send, g1_recv, g0_send, g0_recv, y_send, y_recv, here,
):
    ctx = lax.axis_index("ctx")
    head = lax.axis_index("head")
    n_ctx = lax.axis_size("ctx")
    core = lax.rem(ctx, 2)
    even = core == 0
    odd = core == 1
    group = head // 4
    member = lax.rem(head, 4)

    def at(step):
        return (ctx + step, head)

    def peer(j):
        return (ctx, group * 4 + lax.rem(member + j, 4))

    def remote(src, dst, ss, rs, dev):
        return pltpu.make_async_remote_copy(
            src_ref=src, dst_ref=dst, send_sem=ss, recv_sem=rs,
            device_id=dev, device_id_type=MESH,
        )

    source = (k_hbm, v_hbm)
    cols = pl.ds(pl.multiple_of(group * D, D), D)
    loads = [
        pltpu.make_async_copy(k_hbm.at[:, cols], kv.at[0, 0], in_sem.at[0]),
        pltpu.make_async_copy(v_hbm.at[:, cols], kv.at[0, 1], in_sem.at[1]),
        pltpu.make_async_copy(q_hbm, q_in, in_sem.at[2]),
        pltpu.make_async_copy(do_hbm, do_in, in_sem.at[3]),
        pltpu.make_async_copy(doc_hbm, doc_ref, in_sem.at[4]),
    ]
    for c in loads:
        c.start()

    has = {-2: ctx >= 2, -1: ctx >= 1, 1: ctx < n_ctx - 1, 2: ctx < n_ctx - 2}
    barrier = pltpu.get_barrier_semaphore()
    up, down = member < 3, member > 0

    def beside(step):
        return (ctx, head + step)

    late = (ctx == 0) & (head == 0)
    stand_in = (ctx == 0) & (head == 1)
    fed = (head == 0) & (ctx >= 1) & (ctx <= 2)

    def signal(sem, dev):
        pl.semaphore_signal(sem, inc=1, device_id=dev, device_id_type=MESH)

    @pl.when(has[-1])
    def _():
        signal(barrier, at(-1))

    @pl.when(even & has[-2])
    def _():
        signal(barrier, at(-2))

    @pl.when(up & jnp.logical_not(late))
    def _():
        signal(barrier, beside(1))

    @pl.when(down)
    def _():
        signal(barrier, beside(-1))

    @pl.when(fed)
    def _():
        signal(barrier, (0, 1))

    greeters = (has[1], even & has[2], up, down & jnp.logical_not(stand_in), stand_in, stand_in)
    pl.semaphore_wait(barrier, sum(g.astype(jnp.int32) for g in greeters))

    def hop1(i):
        return remote(source[i].at[:, cols], kv.at[1, i], kv_send.at[0, i], kv_recv.at[1, i], at(1))

    def hop2(i):
        return remote(source[i].at[:, cols], kv.at[2, i], kv_send.at[1, i], kv_recv.at[2, i], at(2))

    def feed(n, i):
        return remote(source[i].at[:, cols], kv.at[n, i], kv_send.at[n + 1, i], kv_recv.at[n, i], (n, 0))

    def relay(i):
        return remote(kv.at[1, i], kv.at[2, i], relay_send.at[i], kv_recv.at[2, i], at(1))

    def recv2(i):
        return remote(kv.at[0, i], kv.at[2, i], kv_send.at[1, i], kv_recv.at[2, i], at(2))

    for i in (0, 1):
        @pl.when(has[1] & jnp.logical_not(late))
        def _(i=i):
            hop1(i).start()

        @pl.when(even & has[2] & jnp.logical_not(late))
        def _(i=i):
            hop2(i).start()

        @pl.when(stand_in)
        def _(i=i):
            feed(1, i).start()
            feed(2, i).start()

    @pl.when(late)
    def _():
        signal(here.at[3], at(1))
        signal(here.at[3], at(2))
        signal(here.at[3], beside(1))

    @pl.when(up & down & jnp.logical_not(stand_in))
    def _():
        signal(here.at[0], beside(-1))
        signal(here.at[1], beside(1))

    loads[2].wait()
    loads[3].wait()
    loads[4].wait()
    loads[0].wait()
    loads[1].wait()
    for half in range(2):
        for h in range(2):
            c = half * T + h * H
            a = q_in[half * H:(half + 1) * H, h * D:(h + 1) * D]
            q2[c:c + H, :] = a
            q_t[:, c:c + H] = a.T
            a = do_in[half * H:(half + 1) * H, h * D:(h + 1) * D]
            do2[c:c + H, :] = a
            do_t[:, c:c + H] = a.T

    doc = doc_ref[0:1, :] - ctx * T

    def score(b):
        for half in range(2):
            lo_k, hi_k = SEEN[b, half]
            n = hi_k - lo_k
            c0 = half * T
            s = dot(kv[b, 0, lo_k:hi_k, :], q2[c0:c0 + T, :], 1, 1) * SCALE2
            key_pos = lax.broadcasted_iota(jnp.int32, (n, H), 0) + (lo_k - b * T)
            query_pos = lax.broadcasted_iota(jnp.int32, (1, H), 1) + half * H
            first = jnp.maximum(query_pos - (WINDOW - 1), doc[:, half * H:(half + 1) * H])
            visible = key_pos >= first
            if b == 0:
                visible = visible & (key_pos <= query_pos)
            visible = jnp.concatenate([visible, visible], axis=1)
            s = jnp.where(visible, s, -1e30)
            m = jnp.max(s, axis=0, keepdims=True)
            if b > 0:
                m_old = m_s[3, 0:1, c0:c0 + T]
                m = jnp.maximum(m_old, m)
            e = jnp.exp2(s - m)
            l = jnp.sum(e, axis=0, keepdims=True)
            if b > 0:
                l = l + jnp.exp2(m_old - m) * l_s[0:1, c0:c0 + T]
            m_s[b, 0:1, c0:c0 + T] = m
            m_s[3, 0:1, c0:c0 + T] = m
            l_s[0:1, c0:c0 + T] = l
            e_s[b, lo_k:hi_k, c0:c0 + T] = e.astype(bf16)

    def dprob(b):
        for half in range(2):
            lo_k, hi_k = SEEN[b, half]
            c0 = half * T
            dp = dot(kv[b, 1, lo_k:hi_k, :], do2[c0:c0 + T, :], 1, 1)
            dp_s[b, lo_k:hi_k, c0:c0 + T] = dp
            e = e_s[b, lo_k:hi_k, c0:c0 + T].astype(f32)
            dl = jnp.sum(e * dp, axis=0, keepdims=True)
            dl = dl * c_s[b, 0:1, c0:c0 + T]
            if b == 0:
                delta_s[0:1, c0:c0 + T] = dl
            else:
                delta_s[0:1, c0:c0 + T] += dl

    def coef(b):
        c_s[b, 0:1, :] = jnp.exp2(m_s[b, 0:1, :] - m_s[3, 0:1, :]) / l_s[0:1, :]

    def assemble(b, p):
        if b == 0:
            return [(0, H, p[0] + p[1][:, :H]), (H, T, p[1][:, H:])]
        if b == 1:
            return [(0, T, p[0] + p[1])]
        return [(0, H, p[0][:, :H]), (H, T, p[0][:, H:] + p[1])]

    def value_part(b):
        w = (do_t[...].astype(f32) * c_s[b, 0:1, :]).astype(bf16)
        parts = []
        for half in range(2):
            lo_k, hi_k = SEEN[b, half]
            c0 = half * T
            parts.append(dot(w[:, c0:c0 + T], e_s[b, lo_k:hi_k, c0:c0 + T], 1, 1))
        return assemble(b, parts)

    def key_part(b):
        w = (q_t[...].astype(f32) * (c_s[b, 0:1, :] * SCALE)).astype(bf16)
        parts = []
        for half in range(2):
            lo_k, hi_k = SEEN[b, half]
            c0 = half * T
            ds = e_s[b, lo_k:hi_k, c0:c0 + T].astype(f32)
            ds = (ds * (dp_s[b, lo_k:hi_k, c0:c0 + T] - delta_s[0:1, c0:c0 + T])).astype(bf16)
            ds_s[b, lo_k:hi_k, c0:c0 + T] = ds
            parts.append(dot(w[:, c0:c0 + T], ds, 1, 1))
        return assemble(b, parts)

    def row_parts(b):
        k_t, v_t = kv[b, 0].T, kv[b, 1].T
        for half in range(2):
            lo_k, hi_k = SEEN[b, half]
            c0 = half * T
            c = c_s[b, 0:1, c0:c0 + T]
            o = dot(v_t[:, lo_k:hi_k], e_s[b, lo_k:hi_k, c0:c0 + T], 1, 0) * c
            dq = dot(k_t[:, lo_k:hi_k], ds_s[b, lo_k:hi_k, c0:c0 + T], 1, 0) * (c * SCALE)
            if b == 0:
                o_acc[:, c0:c0 + T] = o
                dq_s[:, c0:c0 + T] = dq
            else:
                o_acc[:, c0:c0 + T] += o
                dq_s[:, c0:c0 + T] += dq

    def piece(ref, p):
        i, a, z = PIECES[p]
        return ref.at[i, :, pl.ds(a, z - a)]

    def exch(i, step):
        return remote(exch_out.at[i], exch_in.at[i], ex_send.at[i], ex_recv.at[i], at(step))

    def send_g1(p):
        return remote(piece(g1_out, p), piece(g1_in, p), g1_send.at[p], g1_recv.at[p], at(-1))

    def send_g0(p):
        return remote(piece(g0_out, p), piece(g0_in, p), g0_send.at[p], g0_recv.at[p], at(-2))

    def y_copy(p, j):
        i, a, z = PIECES[p]
        to = pl.multiple_of(lax.rem(member + j, 4) * 32, 32)
        return remote(
            y_out.at[i, pl.ds(to, 32), pl.ds(a, z - a)], y_in.at[i, j - 1, :, pl.ds(a, z - a)],
            y_send.at[p, j - 1], y_recv.at[p, j - 1], peer(j),
        )

    def of(i):
        return [p for p in range(3) if PIECES[p][0] == i]

    def tails(b, i, parts):
        if b == 2:
            for a, z, x in parts:
                g0_out[i, :, a:z] = x.astype(bf16)

            @pl.when(even)
            def _():
                for p in of(i):
                    send_g0(p).start()

            @pl.when(odd)
            def _():
                exch_out[i] = g0_out[i]
                exch(i, -1).start()
        else:
            for a, z, x in parts:
                part[i, :, a:z] = x

            @pl.when(odd)
            def _():
                for p in of(i):
                    _, a, z = PIECES[p]
                    g1_out[i, :, a:z] = part[i, :, a:z].astype(bf16)
                    send_g1(p).start()

    def combine(i):
        exch(i, 1).wait_recv()
        for p in of(i):
            _, a, z = PIECES[p]
            g1_out[i, :, a:z] = (part[i, :, a:z] + exch_in[i, :, a:z].astype(f32)).astype(bf16)
            send_g1(p).start()

    score(0)

    @pl.when(has[-1])
    def _():
        hop1(0).wait_recv()

        @pl.when(even)
        def _():
            relay(0).start()
        score(1)

    @pl.when(has[-2])
    def _():
        recv2(0).wait_recv()
        score(2)
        coef(2)

        @pl.when(fed & even)
        def _():
            pl.semaphore_wait(here.at[3], 1)
        tails(2, 1, value_part(2))

    @pl.when(has[-1])
    def _():
        coef(1)

        @pl.when(fed & odd)
        def _():
            pl.semaphore_wait(here.at[3], 1)
        tails(1, 1, value_part(1))

    coef(0)
    dprob(0)

    @pl.when(has[-1])
    def _():
        hop1(1).wait_recv()

        @pl.when(even)
        def _():
            relay(1).start()
        dprob(1)

    @pl.when(has[-2])
    def _():
        @pl.when(even)
        def _():
            combine(1)
        recv2(1).wait_recv()
        dprob(2)
        tails(2, 0, key_part(2))

    @pl.when(has[-1])
    def _():
        tails(1, 0, key_part(1))

        @pl.when(even & has[-2])
        def _():
            combine(0)

    for a, z, x in value_part(0):
        own[1, :, a:z] = x
    for a, z, x in key_part(0):
        own[0, :, a:z] = x

    def finish(p):
        i, a, z = PIECES[p]

        @pl.when(has[1])
        def _():
            send_g1(p).wait_recv()
            own[i, :, a:z] += g1_in[i, :, a:z].astype(f32)

        @pl.when(even & has[2])
        def _():
            send_g0(p).wait_recv()
            own[i, :, a:z] += g0_in[i, :, a:z].astype(f32)
        y_out[i, :, a:z] = own[i, :, a:z].astype(bf16)

        @pl.when(member < 2)
        def _():
            for j in (3, 2, 1):
                y_copy(p, j).start()

        @pl.when(member >= 2)
        def _():
            for j in (1, 2, 3):
                y_copy(p, j).start()

    @pl.when(stand_in)
    def _():
        pl.semaphore_wait(here.at[3], 1)
        signal(here.at[0], beside(-1))
        signal(here.at[1], beside(1))

    @pl.when(member == 1)
    def _():
        pl.semaphore_wait(here.at[0], 1)
        signal(here.at[2], beside(-1))

    @pl.when(member == 2)
    def _():
        pl.semaphore_wait(here.at[1], 1)
        signal(here.at[2], beside(1))

    row_parts(0)

    @pl.when(has[-1])
    def _():
        row_parts(1)

    @pl.when(has[-2])
    def _():
        row_parts(2)

    for half in range(2):
        for h in range(2):
            c = half * T + h * H
            rows, lanes = slice(half * H, (half + 1) * H), slice(h * D, (h + 1) * D)
            o_vm[rows, lanes] = o_acc[:, c:c + H].T.astype(bf16)
            dq_vm[rows, lanes] = dq_s[:, c:c + H].T.astype(bf16)

    @pl.when(member == 0)
    def _():
        pl.semaphore_wait(here.at[0], 1)
        pl.semaphore_wait(here.at[2], 1)

    @pl.when(member == 3)
    def _():
        pl.semaphore_wait(here.at[1], 1)
        pl.semaphore_wait(here.at[2], 1)

    for p in range(3):
        finish(p)

    mine = pl.multiple_of(member * 32, 32)
    for p in range(3):
        i, a, z = PIECES[p]
        acc = own[i, pl.ds(mine, 32), a:z]
        for j in (1, 2, 3):
            y_copy(p, j).wait_recv()
            acc = acc + y_in[i, j - 1, :, a:z].astype(f32)
        (dk_ref, dv_ref)[i][:, a:z] = acc

    for i in (0, 1):
        @pl.when(has[1] & jnp.logical_not(late))
        def _(i=i):
            hop1(i).wait_send()

        @pl.when(even & has[2] & jnp.logical_not(late))
        def _(i=i):
            hop2(i).wait_send()

        @pl.when(stand_in)
        def _(i=i):
            feed(1, i).wait_send()
            feed(2, i).wait_send()

        @pl.when(even & has[-1])
        def _(i=i):
            relay(i).wait_send()

        @pl.when(odd & has[-2])
        def _(i=i):
            exch(i, -1).wait_send()

    for p in range(3):
        @pl.when(has[-1])
        def _(p=p):
            send_g1(p).wait_send()

        @pl.when(even & has[-2])
        def _(p=p):
            send_g0(p).wait_send()
        for j in (1, 2, 3):
            y_copy(p, j).wait_send()


def place(o, dq, dk, dv, o_out, dq_out, dk_out, dv_out, sem):
    pairs = ((o, o_out), (dq, dq_out), (dk, dk_out), (dv, dv_out))
    copies = [pltpu.make_async_copy(a, b, sem.at[i]) for i, (a, b) in enumerate(pairs)]
    for c in copies:
        c.start()
    for c in copies:
        c.wait()


def body(queries, keys, values, out_grad, doc_start):
    hbm = pl.BlockSpec(memory_space=pltpu.HBM)
    vmem = pl.BlockSpec(memory_space=pltpu.VMEM)
    V, DMA = pltpu.VMEM, pltpu.SemaphoreType.DMA
    S = jax.ShapeDtypeStruct
    o, dq, dk, dv = pl.pallas_call(
        kernel,
        out_shape=(S((T, 2 * D), bf16), S((T, 2 * D), bf16), S((32, T), f32), S((32, T), f32)),
        in_specs=[hbm] * 5,
        out_specs=(vmem,)*4,
        scratch_shapes=[
            V((T, 2 * D), bf16), V((T, 2 * D), bf16), V((1, T), jnp.int32), V((3, 2, T, D), bf16),
            V((2 * T, D), bf16), V((2 * T, D), bf16), V((D, 2 * T), bf16), V((D, 2 * T), bf16),
            V((3, T, 2 * T), bf16), V((3, T, 2 * T), f32), V((3, T, 2 * T), bf16),
            V((4, 8, 2 * T), f32), V((8, 2 * T), f32), V((3, 8, 2 * T), f32),
            V((8, 2 * T), f32), V((D, 2 * T), f32), V((D, 2 * T), f32),
            V((2, D, T), f32), V((2, D, T), f32), V((2, D, T), bf16), V((2, D, T), bf16),
            V((2, D, T), bf16), V((2, D, T), bf16), V((2, D, T), bf16), V((2, D, T), bf16),
            V((2, D, T), bf16), V((2, 3, 32, T), bf16),
            DMA((5,)), DMA((4, 2)), DMA((3, 2)), DMA((2,)), DMA((2,)), DMA((2,)),
            DMA((3,)), DMA((3,)), DMA((3,)), DMA((3,)), DMA((3, 3)), DMA((3, 3)),
            pltpu.SemaphoreType.REGULAR((4,)),
        ],
        compiler_params=pltpu.CompilerParams(
            collective_id=0, has_side_effects=True, vmem_limit_bytes=int(53.25 * 2**20)
        ),
    )(queries, keys, values, out_grad, pltpu.with_memory_space_constraint(doc_start.reshape(1, T), pltpu.HBM))
    o, dq, dk, dv = pl.pallas_call(
        place,
        out_shape=(S((T, 2 * D), bf16), S((T, 2 * D), bf16), S((32, T), f32), S((32, T), f32)),
        in_specs=[vmem] * 4,
        out_specs=(hbm,) * 4,
        scratch_shapes=[DMA((4,))],
        compiler_params=pltpu.CompilerParams(vmem_limit_bytes=4 * 2**20),
    )(o, dq, dk, dv)
    return o, dq, dk.T, dv.T


def solution(mesh):
    placed = (P("ctx", "head"), P("ctx", None), P("ctx", None), P("ctx", "head"), P("ctx"))
    return jax.shard_map(
        body,
        mesh=mesh,
        in_specs=placed,
        out_specs=(P("ctx", "head"),) * 4,
        check_vma=False,
    )
```
